32 devices in a mesh: dp: 8 (over z, y), pipe: 2 (over x), tensor: 2 (over core).
Axes of the slice: x: 2, y: 2, z: 4, core: 2. Of those that a mesh axis runs over, the one named last changes fastest.
Arguments:
- hidden: bfloat16 [2, 1024, 8192], P('pipe', 'dp', 'tensor'), may hold values from -6 to 6
- doc_lengths: int32 [2, 8, 8], P('pipe', 'dp'), may hold values from 1 to 32, 128 in all within a row
- doc_target: int32 [2, 8, 8], P('pipe', 'dp'), may hold values from 0 to 7, each once within a row
- norm_gain: float32 [2, 8192], P('pipe'), may hold values from 0.5 to 1.5
- q_weight: bfloat16 [2, 8192, 8192], P('pipe', None, 'tensor'), may hold values from -0.0625 to 0.0625
- kv_weight: bfloat16 [2, 8192, 2048], P('pipe', None, 'tensor'), may hold values from -0.0625 to 0.0625
Outputs:
- balanced: bfloat16 [2, 2048, 8192], P('pipe', 'dp', 'tensor')
The draws below stay inside these ranges and needn't reach their ends.
Inputs may be any that keep to these rules, and one draw needn't show every extreme that they name: `doc_lengths`: each row of lengths sums to 128 and its largest entry is exactly 32. `doc_target`: each row is a permutation of the dp indices.
All inputs are finite; a program needn't handle non-finite values.
Results may differ from the reference program's by a relative error of at most 0.0067.
Values may be sent and summed in bfloat16 or wider, within the bound.
A program may use at most 128 MiB of HBM per device.

```python
import math
from functools import partial
import jax
import jax.numpy as jnp
import numpy as np
from jax import lax

D = 8192
HD = 128
KV_HEADS = 8
TOK_DEV = 128
STEPS = 2
CAPR = 32
TOKENS = 1024
N_DP = 8
N_PIPE = 2


def steps_of(stream_key, dims, cuts, low, largest):
    def one(position, shards_of):
        heights = jax.random.uniform(jax.random.fold_in(jax.random.fold_in(stream_key, 6), position), (shards_of,), jnp.float32, low / len(cuts), largest / len(cuts))
        return jnp.repeat(jnp.exp(heights), dims[position] // shards_of).reshape((-1,) + (1,) * (len(dims) - position - 1))

    loudness = one(*cuts[0])
    for cut in cuts[1:]:
        loudness = loudness * one(*cut)
    return loudness


def split_up(amount, total, limit, slope):
    weights = [(1 << 20) // math.isqrt(standing ** slope) + 1 for standing in range(2, amount + 1)]
    surplus, counts = total - limit - (amount - 1), [1] * (amount - 1)
    while surplus > 0:
        free = [i for i in range(amount - 1) if counts[i] < limit]
        mass, remaining = sum([weights[i] for i in free]), surplus
        for i in free:
            extra = min(limit - counts[i], max(1, remaining * weights[i] // mass), surplus)
            counts[i] = counts[i] + extra
            surplus = surplus - extra
    return np.array([limit] + counts)


def uneven_parts(rng, count, total, most, skew):
    if count == 2:
        one = jax.random.randint(rng, (), max(1, total - most), min(most, total - 1) + 1)
        return jnp.stack([one, total - one])
    sizes = jnp.asarray(split_up(count, total, most, skew), jnp.int32)
    pairs = (count - 1) // 2
    donor, sink = sizes[1:1 + 2 * pairs:2], sizes[2:2 + 2 * pairs:2]
    room = jnp.minimum(donor - 1, most - sink)
    moved = jax.random.randint(jax.random.fold_in(rng, 1), (pairs,), 0, 1 << 20) % (room + 1)
    sizes = sizes.at[1:1 + 2 * pairs:2].set(donor - moved).at[2:2 + 2 * pairs:2].set(sink + moved)
    return sizes[jax.random.permutation(jax.random.fold_in(rng, 2), count)]


def bell_draw(rng, extent, scale, bound, split=(), held_as=jnp.bfloat16):
    array = scale * jax.random.normal(rng, extent, jnp.float32)
    if split:
        array = array * steps_of(rng, extent, split, -0.22, 0.18)
    return jnp.clip(array, -bound, bound).astype(held_as)


def setup_inputs(seed: int = 0) -> dict:
    streams_of = jax.random.split(jax.random.key(seed), 7)
    return {
        "hidden": bell_draw(streams_of[0], (N_PIPE, TOKENS, D), 1.0, 6.0, ((0, 2), (1, 8), (2, 2))),
        "doc_lengths": jax.vmap(lambda own: uneven_parts(own, N_DP, TOK_DEV, CAPR, 2))(jax.random.split(streams_of[1], N_PIPE * N_DP)).reshape((N_PIPE, N_DP, N_DP)).astype(jnp.int32),
        "doc_target": jax.vmap(lambda own: jax.random.permutation(own, N_DP))(jax.random.split(streams_of[2], N_PIPE * N_DP)).reshape((N_PIPE, N_DP, N_DP)).astype(jnp.int32),
        "norm_gain": jnp.clip(1.0 + 0.1 * jax.random.normal(streams_of[3], (N_PIPE, D), jnp.float32), 0.5, 1.5),
        "q_weight": bell_draw(streams_of[4], (N_PIPE, D, D), D ** -0.5, 0.0625, ((0, 2), (2, 2))),
        "kv_weight": bell_draw(streams_of[5], (N_PIPE, D, 2 * KV_HEADS * HD), D ** -0.5, 0.0625, ((0, 2), (2, 2))),
    }


def build_send(token_rows, lengths, targets, capacity, groups):
    ordinal = jnp.arange(groups, dtype=jnp.int32)
    offsets = jnp.cumsum(lengths) - lengths
    onehot = (targets[None, :] == ordinal[:, None]).astype(jnp.int32)
    doc_sizes = lax.optimization_barrier(jnp.sum(onehot * lengths[None, :], axis=1))
    doc_starts = lax.optimization_barrier(jnp.sum(onehot * offsets[None, :], axis=1))
    within = jnp.arange(capacity, dtype=jnp.int32)
    row_index = jnp.minimum(doc_starts[:, None] + within[None, :], token_rows.shape[0] - 1).astype(jnp.int32)
    picked = jnp.take(token_rows, row_index.reshape(-1), axis=0).reshape(groups, capacity, token_rows.shape[1])
    inside = within[None, :] < doc_sizes[:, None]
    return (jnp.where(inside[:, :, None], picked, jnp.zeros_like(picked)), doc_sizes)

def ref_layer(current, gain_row, query_weight, pair_weight, allowed):
    blocks, length, features = current.shape
    per_group = D // HD // KV_HEADS
    widened = current.astype(jnp.float32)
    total_sq = lax.optimization_barrier(jnp.sum(widened * widened, axis=-1))
    scale_row = lax.rsqrt(total_sq / D + 1e-05)
    normed = (widened * scale_row[..., None] * gain_row).astype(jnp.bfloat16)
    flat_rows = normed.reshape(blocks * length, features)
    queries = jnp.dot(flat_rows, query_weight, preferred_element_type=jnp.float32).astype(jnp.bfloat16)
    key_value = jnp.dot(flat_rows, pair_weight, preferred_element_type=jnp.float32).astype(jnp.bfloat16)
    queries = queries.reshape(blocks, length, KV_HEADS, per_group, HD).astype(jnp.float32)
    key_value = key_value.reshape(blocks, length, 2, HD, KV_HEADS).astype(jnp.float32)
    key_rows = key_value[:, :, 0]
    values = key_value[:, :, 1]
    scores = jnp.einsum('bqgph,bkhg->bgpqk', queries, key_rows) * HD ** (-0.5)
    exp_scores = jnp.where(allowed[:, None, None], jnp.exp(scores), 0.0)
    probabilities = (exp_scores / lax.optimization_barrier(jnp.sum(exp_scores, axis=-1, keepdims=True))).astype(jnp.bfloat16)
    attended = jnp.einsum('bgpqk,bkhg->bqgph', probabilities.astype(jnp.float32), values)
    attended = attended.reshape(blocks, length, features)
    return (widened + attended).astype(jnp.bfloat16)

def reference(hidden, doc_lengths, doc_target, norm_gain, q_weight, kv_weight):
    results = []
    within = jnp.arange(TOK_DEV, dtype=jnp.int32)
    causal = within[:, None] >= within[None, :]
    for micro_batch in range(N_PIPE):
        lengths = doc_lengths[micro_batch]
        targets = doc_target[micro_batch]
        current = hidden[micro_batch].reshape(N_DP, TOK_DEV, D)
        doc_ends = jnp.cumsum(lengths, axis=1)
        segment = lax.optimization_barrier(jnp.sum((within[None, :, None] >= doc_ends[:, None, :]).astype(jnp.int32), axis=2))
        allowed = (segment[:, :, None] == segment[:, None, :]) & causal[None]
        for layer_step in range(STEPS):
            section_index = (micro_batch + layer_step) % N_PIPE
            current = ref_layer(current, norm_gain[section_index], q_weight[section_index], kv_weight[section_index], allowed)
        packed, doc_sizes = jax.vmap(partial(build_send, capacity=CAPR, groups=N_DP))(current, lengths, targets)
        results.append(jnp.transpose(packed, (1, 0, 2, 3)).reshape(N_DP * N_DP * CAPR, D))
    stacked = jnp.stack(results)
    return jnp.roll(stacked, STEPS - 1, axis=0)
```

```python
import functools

import jax
import jax.numpy as jnp
from jax import lax
from jax.experimental import pallas as pl
from jax.experimental.pallas import tpu as pltpu
from jax.sharding import PartitionSpec as P

D = 8192
HD = 128
KV_HEADS = 8
STEPS = 2


def passed_along(block, axis, distance):
    devices = range(lax.axis_size(axis))
    route = [((i - distance) % len(devices), i) for i in devices]
    return lax.ppermute(block, axis, route)


def build_send(token_rows, lengths, targets, capacity, groups):
    ordinal = jnp.arange(groups, dtype=jnp.int32)
    offsets = jnp.cumsum(lengths) - lengths
    onehot = (targets[None, :] == ordinal[:, None]).astype(jnp.int32)
    doc_sizes = jnp.sum(onehot * lengths[None, :], axis=1)
    doc_starts = jnp.sum(onehot * offsets[None, :], axis=1)
    within = jnp.arange(capacity, dtype=jnp.int32)
    row_index = jnp.minimum(doc_starts[:, None] + within[None, :], token_rows.shape[0] - 1)
    picked = jnp.take(token_rows, row_index.reshape(-1), axis=0).reshape(
        groups, capacity, token_rows.shape[1]
    )
    inside = within[None, :] < doc_sizes[:, None]
    return (jnp.where(inside[:, :, None], picked, jnp.zeros_like(picked)), doc_sizes)


def doc_masks(lengths, length):
    within = jnp.arange(length, dtype=jnp.int32)
    doc_ends = jnp.cumsum(lengths)
    segment = jnp.sum((within[:, None] >= doc_ends[None, :]).astype(jnp.int32), axis=1)
    causal = within[:, None] >= within[None, :]
    return (segment[:, None] == segment[None, :]) & causal


def attend_heads(queries, kv_local, allowed, local_rank):
    row_count = queries.shape[0]
    local_heads = queries.shape[1] // HD
    per_group = D // HD // KV_HEADS
    kv_count = max(1, local_heads // per_group)
    kv_first = local_rank * local_heads // per_group
    kv_whole = lax.all_gather(kv_local, "tensor", axis=1, tiled=True)
    kv_heads = kv_whole.reshape(row_count, 2, HD, KV_HEADS)
    own_heads = lax.dynamic_slice_in_dim(kv_heads, kv_first, kv_count, 3)
    key_rows = own_heads[:, 0]
    values = own_heads[:, 1]
    grouped = queries.reshape(row_count, kv_count, local_heads // kv_count, HD)
    scores = jnp.einsum(
        "qcph,khc->cpqk", grouped, key_rows, preferred_element_type=jnp.float32
    ) * HD ** (-0.5)
    exp_scores = jnp.where(allowed[None, None], jnp.exp(scores), 0.0)
    probabilities = (exp_scores / jnp.sum(exp_scores, axis=-1, keepdims=True)).astype(jnp.bfloat16)
    attended = jnp.einsum(
        "cpqk,khc->qcph", probabilities, values, preferred_element_type=jnp.float32
    )
    return attended.reshape(row_count, queries.shape[1])


def layer_pass(current, gain_full, query_cols, kv_cols, allowed):
    local_rank = lax.axis_index("tensor")
    widened = current.astype(jnp.float32)
    whole = lax.all_gather(current, "tensor", axis=1, tiled=True)
    whole_wide = whole.astype(jnp.float32)
    scale_row = lax.rsqrt(jnp.sum(whole_wide * whole_wide, axis=-1) / D + 1e-05)
    normed_full = (whole_wide * scale_row[:, None] * gain_full).astype(jnp.bfloat16)
    query_sum = jnp.dot(normed_full, query_cols, preferred_element_type=jnp.float32)
    kv_sum = jnp.dot(normed_full, kv_cols, preferred_element_type=jnp.float32)
    queries = query_sum.astype(jnp.bfloat16)
    kv_local = kv_sum.astype(jnp.bfloat16)
    attended = attend_heads(queries, kv_local, allowed, local_rank)
    return (widened + attended).astype(jnp.bfloat16)


def on_device(hidden, doc_lengths, doc_target, norm_gain, q_weight, kv_weight):
    groups = lax.axis_size("dp")
    current = hidden[0]
    lengths = doc_lengths[0, 0]
    targets = doc_target[0, 0]
    capacity = current.shape[0] // 4
    gain_full = norm_gain[0]
    query_cols = q_weight[0]
    kv_cols = kv_weight[0]
    carried = jnp.stack([lengths, targets]).astype(jnp.bfloat16)
    for layer_step in range(STEPS):
        allowed = doc_masks(carried[0].astype(jnp.int32), current.shape[0])
        current = layer_pass(current, gain_full, query_cols, kv_cols, allowed)
        if layer_step + 1 < STEPS:
            current, carried = passed_along((current, carried), "pipe", 1)
    final_lengths = carried[0].astype(jnp.int32)
    final_targets = carried[1].astype(jnp.int32)
    packed, doc_sizes = build_send(current, final_lengths, final_targets, capacity, groups)
    received = lax.all_to_all(packed, "dp", split_axis=0, concat_axis=0, tiled=True)
    return received.reshape(1, groups * capacity, received.shape[2])


CHUNK = 256
SLOTS = 6


def fused_kernel(
    sizes, hidden, meta, gain, wq, wkv, out,
    x_own, x_other, h_send, next_own, next_other, meta_next, normed, spread, kv_cols,
    kv_send, kv_heads, kv_weights, ring, mask, chooser, q_held, packed,
    sem_x, sem_xs, sem_xr, sem_ms, sem_mr, sem_kvw, sem_ring, sem_kvs, sem_kvr,
    sem_hs, sem_hr, sem_fs, sem_fr, sem_as, sem_ar, sem_own,
):
    n_dp, n_pipe, docs = sizes
    rows, width = hidden.shape
    features = gain.shape[1]
    n_chunks = width // CHUNK
    kv_chunks = wkv.shape[1] // CHUNK
    own_kv = kv_heads.shape[2]
    chunk_heads = CHUNK // HD
    group_chunks = n_chunks // own_kv
    capacity = packed.shape[1]
    dp = lax.axis_index("dp")
    pipe = lax.axis_index("pipe")
    side = lax.axis_index("tensor")
    other = 1 - side
    following = lax.rem(pipe + 1, n_pipe)
    preceding = lax.rem(pipe + n_pipe - 1, n_pipe)
    total = STEPS * n_chunks

    def cols(j):
        return pl.ds(pl.multiple_of(j * CHUNK, CHUNK), CHUNK)

    def kv_copy(n):
        return pltpu.make_async_copy(wkv.at[:, cols(n)], kv_weights.at[n], sem_kvw.at[n])

    def ring_copy(c):
        slot = lax.rem(c, SLOTS)
        return pltpu.make_async_copy(
            wq.at[:, cols(lax.rem(c, n_chunks))], ring.at[slot], sem_ring.at[slot]
        )

    def x_copy(j):
        return pltpu.make_async_copy(hidden.at[:, cols(j)], x_own.at[j], sem_x.at[j])

    def x_remote(j):
        return pltpu.make_async_remote_copy(
            hidden.at[:, cols(j)], x_other.at[j], sem_xs.at[j], sem_xr.at[j],
            device_id={"tensor": other}, device_id_type=pl.DeviceIdType.MESH,
        )

    def meta_remote():
        return pltpu.make_async_remote_copy(
            meta, meta_next, sem_ms, sem_mr,
            device_id={"pipe": following}, device_id_type=pl.DeviceIdType.MESH,
        )

    def kv_remote(layer):
        return pltpu.make_async_remote_copy(
            kv_send.at[layer], kv_heads.at[layer, side], sem_kvs.at[layer], sem_kvr.at[layer],
            device_id={"tensor": other}, device_id_type=pl.DeviceIdType.MESH,
        )

    def h_remote(j):
        return pltpu.make_async_remote_copy(
            h_send.at[j], next_own.at[j], sem_hs.at[j], sem_hr.at[j],
            device_id={"pipe": following}, device_id_type=pl.DeviceIdType.MESH,
        )

    def forward_remote(j):
        return pltpu.make_async_remote_copy(
            next_own.at[j], next_other.at[j], sem_fs.at[j], sem_fr.at[j],
            device_id={"tensor": other}, device_id_type=pl.DeviceIdType.MESH,
        )

    def doc_rows(index):
        return pl.ds(pl.multiple_of(index * capacity, capacity), capacity)

    def doc_remote(away, j):
        target = lax.rem(dp + away, n_dp)
        return pltpu.make_async_remote_copy(
            packed.at[target, :, cols(j)], out.at[doc_rows(dp), cols(j)],
            sem_as.at[away], sem_ar.at[away],
            device_id={"dp": target}, device_id_type=pl.DeviceIdType.MESH,
        )

    def doc_all(away):
        target = lax.rem(dp + away, n_dp)
        source = lax.rem(dp + n_dp - away, n_dp)
        return pltpu.make_async_remote_copy(
            packed.at[target], out.at[doc_rows(source)],
            sem_as.at[away], sem_ar.at[away],
            device_id={"dp": target}, device_id_type=pl.DeviceIdType.MESH,
        )

    for j in range(n_chunks):
        x_copy(j).start()
    for n in range(kv_chunks):
        kv_copy(n).start()
    for c in range(SLOTS):
        ring_copy(c).start()

    barrier = pltpu.get_barrier_semaphore()
    pl.semaphore_signal(
        barrier, inc=1, device_id={"tensor": other}, device_id_type=pl.DeviceIdType.MESH
    )
    pl.semaphore_signal(
        barrier, inc=1, device_id={"pipe": following}, device_id_type=pl.DeviceIdType.MESH
    )
    greeted = n_dp + 1
    if n_pipe > 2:
        pl.semaphore_signal(
            barrier, inc=1, device_id={"pipe": preceding}, device_id_type=pl.DeviceIdType.MESH
        )
        greeted += 1
    for away in range(1, n_dp):
        pl.semaphore_signal(
            barrier, inc=1, device_id={"dp": lax.rem(dp + away, n_dp)},
            device_id_type=pl.DeviceIdType.MESH,
        )
    pl.semaphore_wait(barrier, greeted)
    for j in range(n_chunks):
        x_remote(j).start()
    meta_remote().start()

    n_kv = kv_cols.shape[1]
    cols_wide = spread.shape[0]
    out_col = lax.broadcasted_iota(jnp.int32, (128, n_kv), 1)
    wanted = lax.rem(out_col, HD) * KV_HEADS + out_col // HD

    def fill_spread(i, carry):
        base = pl.multiple_of(i * 128, 128)
        row = lax.broadcasted_iota(jnp.int32, (128, n_kv), 0) + base
        spread[pl.ds(base, 128), :] = (row == wanted).astype(jnp.float32).astype(jnp.bfloat16)
        return carry

    lax.fori_loop(0, cols_wide // 128, fill_spread, 0)

    def fill_mask(source):
        row = lax.broadcasted_iota(jnp.int32, (rows, rows), 0)
        col = lax.broadcasted_iota(jnp.int32, (rows, rows), 1)
        row_doc = jnp.zeros((rows, rows), jnp.int32)
        col_doc = jnp.zeros((rows, rows), jnp.int32)
        end = jnp.zeros((1, 1), jnp.int32)
        for d in range(docs):
            end = end + source[0:1, d:d + 1]
            row_doc = row_doc + (row >= end).astype(jnp.int32)
            col_doc = col_doc + (col >= end).astype(jnp.int32)
        allowed = jnp.where((row_doc == col_doc) & (row >= col), 1.0, 0.0)
        for i in range(chunk_heads):
            mask[i * rows:(i + 1) * rows, :] = allowed

    def fill_chooser(source):
        row = lax.broadcasted_iota(jnp.int32, (1, rows), 1)
        goal = jnp.full((1, rows), -1, jnp.int32)
        begin = jnp.zeros((1, 1), jnp.int32)
        for d in range(docs):
            end = begin + source[0:1, d:d + 1]
            place = source[1:2, d:d + 1] * capacity + row - begin
            goal = jnp.where((row >= begin) & (row < end), place, goal)
            begin = end
        slot = lax.broadcasted_iota(jnp.int32, (n_dp * capacity, rows), 0)
        chooser[...] = (slot == goal).astype(jnp.float32).astype(jnp.bfloat16)

    def normalise(mine, theirs):
        def squares(j, acc):
            a = mine[j].astype(jnp.float32)
            b = theirs[j].astype(jnp.float32)
            return acc + a * a + b * b

        acc = lax.fori_loop(0, n_chunks, squares, jnp.zeros((rows, CHUNK), jnp.float32))
        scale = lax.rsqrt(jnp.sum(acc, axis=-1, keepdims=True) / features + 1e-05)

        def write(j, carry):
            for held, half in ((mine, side), (theirs, other)):
                where = cols(half * n_chunks + j)
                wide = held[j].astype(jnp.float32) * scale * gain[:, where]
                normed[:, where] = wide.astype(jnp.bfloat16)
            return carry

        lax.fori_loop(0, n_chunks, write, 0)

    def keys_values(layer):
        def one(n, carry):
            if layer == 0:
                kv_copy(n).wait()
            kv_cols[:, cols(n)] = jnp.dot(
                normed[...], kv_weights[n], preferred_element_type=jnp.float32
            ).astype(jnp.bfloat16)
            return carry

        lax.fori_loop(0, kv_chunks, one, 0)
        for which, keep in ((other, False), (side, True)):
            first = pl.multiple_of(which * own_kv * HD, own_kv * HD)
            heads = jnp.dot(
                kv_cols[...], spread[:, pl.ds(first, own_kv * HD)],
                preferred_element_type=jnp.float32,
            ).astype(jnp.bfloat16)
            for g in range(own_kv):
                if keep:
                    kv_heads[layer, side, g] = heads[:, g * HD:(g + 1) * HD]
                else:
                    kv_send[layer, g] = heads[:, g * HD:(g + 1) * HD]
            if not keep:
                kv_remote(layer).start()

    def query(c):
        return jnp.dot(
            normed[...], ring[lax.rem(c, SLOTS)], preferred_element_type=jnp.float32
        ).astype(jnp.bfloat16)

    def attend(layer, j, mine):
        q = q_held[lax.rem(j, 2)]
        g = j // group_chunks
        stacked = jnp.concatenate([q[:, i * HD:(i + 1) * HD] for i in range(chunk_heads)], axis=0)
        scores = lax.dot_general(
            stacked, kv_heads[layer, 0, g], (((1,), (1,)), ((), ())),
            preferred_element_type=jnp.float32,
        ) * HD ** (-0.5)
        e = jnp.where(mask[...] > 0.0, jnp.exp(scores), 0.0)
        p = (e * (1.0 / jnp.sum(e, axis=-1, keepdims=True))).astype(jnp.bfloat16)
        a = jnp.dot(p, kv_heads[layer, 1, g], preferred_element_type=jnp.float32)
        side_by_side = jnp.concatenate(
            [a[i * rows:(i + 1) * rows] for i in range(chunk_heads)], axis=1
        )
        return (mine[j].astype(jnp.float32) + side_by_side).astype(jnp.bfloat16)

    def refill(c):
        @pl.when(c + SLOTS < total)
        def _():
            ring_copy(c + SLOTS).start()

    def run_layer(layer, mine, finish):
        base = layer * n_chunks
        ring_copy(base).wait()
        q_held[0] = query(base)
        refill(jnp.int32(base))
        kv_remote(layer).wait()

        def one(j, carry):
            c = base + j
            ring_copy(c).wait()
            fresh = query(c)
            done = attend(layer, j - 1, mine)
            q_held[lax.rem(j, 2)] = fresh
            refill(c)
            finish(j - 1, done)
            return carry

        lax.fori_loop(1, n_chunks, one, 0)
        finish(n_chunks - 1, attend(layer, n_chunks - 1, mine))

    lag = 4

    def pass_on(j):
        h_remote(j).wait_recv()
        forward_remote(j).start()

    def send_next(j, done):
        h_send[j] = done
        h_remote(j).start()

        @pl.when(j >= lag)
        def _():
            pass_on(j - lag)

    def send_docs(j, done):
        picked = jnp.dot(chooser[...], done, preferred_element_type=jnp.float32)
        picked = picked.astype(jnp.bfloat16)
        for i in range(n_dp):
            packed[i, :, cols(j)] = picked[i * capacity:(i + 1) * capacity]
        for away in range(1, n_dp):
            doc_remote(away, j).start()

    fill_mask(meta)
    for j in range(n_chunks):
        x_copy(j).wait()
    for j in range(n_chunks):
        x_remote(j).wait()
    normalise(x_own, x_other)
    keys_values(0)
    run_layer(0, x_own, send_next)
    for j in range(n_chunks - lag, n_chunks):
        pass_on(j)
    meta_remote().wait()
    fill_mask(meta_next)
    fill_chooser(meta_next)
    for j in range(n_chunks):
        forward_remote(j).wait()
    normalise(next_own, next_other)
    keys_values(1)
    run_layer(1, next_own, send_docs)
    mine = pltpu.make_async_copy(packed.at[dp], out.at[doc_rows(dp)], sem_own)
    mine.start()
    for j in range(n_chunks):
        h_remote(j).wait_send()
    mine.wait()
    for away in range(1, n_dp):
        doc_all(away).wait()


def fused_device(sizes, hidden, doc_lengths, doc_target, norm_gain, q_weight, kv_weight):
    n_dp, n_pipe, docs = sizes
    rows, width = hidden.shape[1:]
    features = norm_gain.shape[1]
    n_chunks = width // CHUNK
    n_kv = kv_weight.shape[2]
    kv_chunks = n_kv // CHUNK
    own_kv = KV_HEADS // 2
    capacity = rows // 4
    chunk_heads = CHUNK // HD
    meta = jnp.zeros((8, 128), jnp.int32)
    meta = meta.at[0, :docs].set(doc_lengths[0, 0]).at[1, :docs].set(doc_target[0, 0])
    bf16 = jnp.bfloat16
    dma = pltpu.SemaphoreType.DMA
    vmem = pltpu.VMEM
    blocks = vmem((n_chunks, rows, CHUNK), bf16)
    result = pl.pallas_call(
        functools.partial(fused_kernel, sizes),
        out_shape=jax.ShapeDtypeStruct((n_dp * capacity, width), bf16),
        in_specs=[
            pl.BlockSpec(memory_space=pl.ANY),
            pl.BlockSpec(memory_space=pltpu.VMEM),
            pl.BlockSpec(memory_space=pltpu.VMEM),
            pl.BlockSpec(memory_space=pl.ANY),
            pl.BlockSpec(memory_space=pl.ANY),
        ],
        out_specs=pl.BlockSpec(memory_space=pl.ANY),
        scratch_shapes=[
            blocks, blocks, blocks, blocks, blocks,
            vmem((8, 128), jnp.int32),
            vmem((rows, features), bf16),
            vmem((n_kv, n_kv), bf16),
            vmem((rows, n_kv), bf16),
            vmem((STEPS, own_kv, rows, HD), bf16),
            vmem((STEPS, 2, own_kv, rows, HD), bf16),
            vmem((kv_chunks, features, CHUNK), bf16),
            vmem((SLOTS, features, CHUNK), bf16),
            vmem((chunk_heads * rows, rows), jnp.float32),
            vmem((n_dp * capacity, rows), bf16),
            vmem((2, rows, CHUNK), bf16),
            vmem((n_dp, capacity, width), bf16),
            dma((n_chunks,)), dma((n_chunks,)), dma((n_chunks,)), dma, dma,
            dma((kv_chunks,)), dma((SLOTS,)), dma((STEPS,)), dma((STEPS,)),
            dma((n_chunks,)), dma((n_chunks,)), dma((n_chunks,)), dma((n_chunks,)),
            dma((n_dp,)), dma((n_dp,)), dma,
        ],
        compiler_params=pltpu.CompilerParams(
            collective_id=0, has_side_effects=True, vmem_limit_bytes=66 * 1024 * 1000
        ),
    )(hidden[0], meta, norm_gain, q_weight[0], kv_weight[0])
    return result[None]


def solution(mesh):
    placed = (
        P("pipe", "dp", "tensor"),
        P("pipe", "dp", None),
        P("pipe", "dp", None),
        P("pipe", None),
        P("pipe", None, "tensor"),
        P("pipe", None, "tensor"),
    )
    run = on_device
    if mesh.shape["tensor"] == 2:
        sizes = (mesh.shape["dp"], mesh.shape["pipe"], mesh.shape["dp"])
        run = functools.partial(fused_device, sizes)
    return jax.shard_map(
        run, mesh=mesh, in_specs=placed, out_specs=P("pipe", "dp", "tensor"), check_vma=False
    )
```

```python
import functools

import jax
import jax.numpy as jnp
from jax import lax
from jax.experimental import pallas as pl
from jax.experimental.pallas import tpu as pltpu
from jax.sharding import PartitionSpec as P

D = 8192
HD = 128
KV_HEADS = 8
STEPS = 2


def passed_along(block, axis, distance):
    devices = range(lax.axis_size(axis))
    route = [((i - distance) % len(devices), i) for i in devices]
    return lax.ppermute(block, axis, route)


def build_send(token_rows, lengths, targets, capacity, groups):
    ordinal = jnp.arange(groups, dtype=jnp.int32)
    offsets = jnp.cumsum(lengths) - lengths
    onehot = (targets[None, :] == ordinal[:, None]).astype(jnp.int32)
    doc_sizes = jnp.sum(onehot * lengths[None, :], axis=1)
    doc_starts = jnp.sum(onehot * offsets[None, :], axis=1)
    within = jnp.arange(capacity, dtype=jnp.int32)
    row_index = jnp.minimum(doc_starts[:, None] + within[None, :], token_rows.shape[0] - 1)
    picked = jnp.take(token_rows, row_index.reshape(-1), axis=0).reshape(
        groups, capacity, token_rows.shape[1]
    )
    inside = within[None, :] < doc_sizes[:, None]
    return (jnp.where(inside[:, :, None], picked, jnp.zeros_like(picked)), doc_sizes)


def doc_masks(lengths, length):
    within = jnp.arange(length, dtype=jnp.int32)
    doc_ends = jnp.cumsum(lengths)
    segment = jnp.sum((within[:, None] >= doc_ends[None, :]).astype(jnp.int32), axis=1)
    causal = within[:, None] >= within[None, :]
    return (segment[:, None] == segment[None, :]) & causal


def attend_heads(queries, kv_local, allowed, local_rank):
    row_count = queries.shape[0]
    local_heads = queries.shape[1] // HD
    per_group = D // HD // KV_HEADS
    kv_count = max(1, local_heads // per_group)
    kv_first = local_rank * local_heads // per_group
    kv_whole = lax.all_gather(kv_local, "tensor", axis=1, tiled=True)
    kv_heads = kv_whole.reshape(row_count, 2, HD, KV_HEADS)
    own_heads = lax.dynamic_slice_in_dim(kv_heads, kv_first, kv_count, 3)
    key_rows = own_heads[:, 0]
    values = own_heads[:, 1]
    grouped = queries.reshape(row_count, kv_count, local_heads // kv_count, HD)
    scores = jnp.einsum(
        "qcph,khc->cpqk", grouped, key_rows, preferred_element_type=jnp.float32
    ) * HD ** (-0.5)
    exp_scores = jnp.where(allowed[None, None], jnp.exp(scores), 0.0)
    probabilities = (exp_scores / jnp.sum(exp_scores, axis=-1, keepdims=True)).astype(jnp.bfloat16)
    attended = jnp.einsum(
        "cpqk,khc->qcph", probabilities, values, preferred_element_type=jnp.float32
    )
    return attended.reshape(row_count, queries.shape[1])


def layer_pass(current, gain_full, query_cols, kv_cols, allowed):
    local_rank = lax.axis_index("tensor")
    widened = current.astype(jnp.float32)
    whole = lax.all_gather(current, "tensor", axis=1, tiled=True)
    whole_wide = whole.astype(jnp.float32)
    scale_row = lax.rsqrt(jnp.sum(whole_wide * whole_wide, axis=-1) / D + 1e-05)
    normed_full = (whole_wide * scale_row[:, None] * gain_full).astype(jnp.bfloat16)
    query_sum = jnp.dot(normed_full, query_cols, preferred_element_type=jnp.float32)
    kv_sum = jnp.dot(normed_full, kv_cols, preferred_element_type=jnp.float32)
    queries = query_sum.astype(jnp.bfloat16)
    kv_local = kv_sum.astype(jnp.bfloat16)
    attended = attend_heads(queries, kv_local, allowed, local_rank)
    return (widened + attended).astype(jnp.bfloat16)


def on_device(hidden, doc_lengths, doc_target, norm_gain, q_weight, kv_weight):
    groups = lax.axis_size("dp")
    current = hidden[0]
    lengths = doc_lengths[0, 0]
    targets = doc_target[0, 0]
    capacity = current.shape[0] // 4
    gain_full = norm_gain[0]
    query_cols = q_weight[0]
    kv_cols = kv_weight[0]
    carried = jnp.stack([lengths, targets]).astype(jnp.bfloat16)
    for layer_step in range(STEPS):
        allowed = doc_masks(carried[0].astype(jnp.int32), current.shape[0])
        current = layer_pass(current, gain_full, query_cols, kv_cols, allowed)
        if layer_step + 1 < STEPS:
            current, carried = passed_along((current, carried), "pipe", 1)
    final_lengths = carried[0].astype(jnp.int32)
    final_targets = carried[1].astype(jnp.int32)
    packed, doc_sizes = build_send(current, final_lengths, final_targets, capacity, groups)
    received = lax.all_to_all(packed, "dp", split_axis=0, concat_axis=0, tiled=True)
    return received.reshape(1, groups * capacity, received.shape[2])


CHUNK = 256
SLOTS = 6


def fused_kernel(
    sizes, hidden, meta, gain, wq, wkv, out,
    x_own, x_other, h_send, next_own, next_other, early_own, early_other, early_send,
    meta_next, meta_early, normed, spread, kv_cols,
    kv_send, kv_heads, kv_weights, ring, mask, early_mask, valid, early_chooser, late_chooser,
    q_held, packed, early_out,
    sem_x, sem_xs, sem_xr, sem_ms, sem_mr, sem_kvw, sem_ring, sem_kvs, sem_kvr,
    sem_hs, sem_hr, sem_fs, sem_fr, sem_as, sem_ar, sem_own,
    sem_es, sem_er, sem_gs, sem_gr, sem_mes, sem_mer,
):
    n_dp, n_pipe, docs = sizes
    rows, width = hidden.shape
    features = gain.shape[1]
    n_chunks = width // CHUNK
    kv_chunks = wkv.shape[1] // CHUNK
    own_kv = kv_heads.shape[2]
    chunk_heads = CHUNK // HD
    group_chunks = n_chunks // own_kv
    half, capacity = packed.shape[:2]
    early_rows = half * capacity
    dp = lax.axis_index("dp")
    pipe = lax.axis_index("pipe")
    side = lax.axis_index("tensor")
    other = 1 - side
    following = lax.rem(pipe + 1, n_pipe)
    preceding = lax.rem(pipe + n_pipe - 1, n_pipe)
    total = STEPS * n_chunks
    layer_rows = (rows, rows + early_rows)
    parity = lax.rem(dp, 2)
    slot_own = dp // 2

    def cols(j):
        return pl.ds(pl.multiple_of(j * CHUNK, CHUNK), CHUNK)

    def kv_copy(n):
        return pltpu.make_async_copy(wkv.at[:, cols(n)], kv_weights.at[n], sem_kvw.at[n])

    def ring_copy(c):
        slot = lax.rem(c, SLOTS)
        return pltpu.make_async_copy(
            wq.at[:, cols(lax.rem(c, n_chunks))], ring.at[slot], sem_ring.at[slot]
        )

    def x_copy(j):
        return pltpu.make_async_copy(hidden.at[:, cols(j)], x_own.at[j], sem_x.at[j])

    def x_remote(j):
        return pltpu.make_async_remote_copy(
            hidden.at[:, cols(j)], x_other.at[j], sem_xs.at[j], sem_xr.at[j],
            device_id={"tensor": other}, device_id_type=pl.DeviceIdType.MESH,
        )

    def meta_remote():
        return pltpu.make_async_remote_copy(
            meta, meta_next, sem_ms, sem_mr,
            device_id={"pipe": following}, device_id_type=pl.DeviceIdType.MESH,
        )

    def meta_on(k):
        return pltpu.make_async_remote_copy(
            meta_next, meta_early.at[slot_own], sem_mes.at[k], sem_mer.at[k],
            device_id={"dp": lax.rem(dp + 2 * k, n_dp)}, device_id_type=pl.DeviceIdType.MESH,
        )

    def meta_in(k):
        source = lax.rem(dp + n_dp - 2 * k, n_dp)
        return pltpu.make_async_remote_copy(
            meta_next, meta_early.at[source // 2], sem_mes.at[k], sem_mer.at[k],
            device_id={"dp": lax.rem(dp + 2 * k, n_dp)}, device_id_type=pl.DeviceIdType.MESH,
        )

    def slot_rows(slot):
        return pl.ds(pl.multiple_of(slot * capacity, capacity), capacity)

    def early_remote(k, j):
        target = lax.rem(dp + 2 * k, n_dp)
        return pltpu.make_async_remote_copy(
            early_send.at[j, target // 2], early_own.at[j, slot_rows(slot_own)],
            sem_es.at[k, j], sem_er.at[k, j],
            device_id={"dp": target}, device_id_type=pl.DeviceIdType.MESH,
        )

    def early_in(k, j):
        target = lax.rem(dp + 2 * k, n_dp)
        source = lax.rem(dp + n_dp - 2 * k, n_dp)
        return pltpu.make_async_remote_copy(
            early_send.at[j, target // 2], early_own.at[j, slot_rows(source // 2)],
            sem_es.at[k, j], sem_er.at[k, j],
            device_id={"dp": target}, device_id_type=pl.DeviceIdType.MESH,
        )

    def early_forward(j):
        return pltpu.make_async_remote_copy(
            early_own.at[j], early_other.at[j], sem_gs.at[j], sem_gr.at[j],
            device_id={"tensor": other}, device_id_type=pl.DeviceIdType.MESH,
        )

    def kv_remote(layer):
        here = pl.ds(0, layer_rows[layer])
        return pltpu.make_async_remote_copy(
            kv_send.at[layer, :, here], kv_heads.at[layer, side, :, here], sem_kvs.at[layer], sem_kvr.at[layer],
            device_id={"tensor": other}, device_id_type=pl.DeviceIdType.MESH,
        )

    def h_remote(j):
        return pltpu.make_async_remote_copy(
            h_send.at[j], next_own.at[j], sem_hs.at[j], sem_hr.at[j],
            device_id={"pipe": following}, device_id_type=pl.DeviceIdType.MESH,
        )

    def forward_remote(j):
        return pltpu.make_async_remote_copy(
            next_own.at[j], next_other.at[j], sem_fs.at[j], sem_fr.at[j],
            device_id={"tensor": other}, device_id_type=pl.DeviceIdType.MESH,
        )

    def doc_rows(index):
        return pl.ds(pl.multiple_of(index * capacity, capacity), capacity)

    def doc_remote(away, j):
        target = lax.rem(dp + away, n_dp)
        return pltpu.make_async_remote_copy(
            packed.at[target // 2, :, cols(j)], out.at[doc_rows(dp), cols(j)],
            sem_as.at[away], sem_ar.at[away],
            device_id={"dp": target}, device_id_type=pl.DeviceIdType.MESH,
        )

    def doc_all(away):
        target = lax.rem(dp + away, n_dp)
        source = lax.rem(dp + n_dp - away, n_dp)
        return pltpu.make_async_remote_copy(
            packed.at[target // 2], out.at[doc_rows(source)],
            sem_as.at[away], sem_ar.at[away],
            device_id={"dp": target}, device_id_type=pl.DeviceIdType.MESH,
        )

    def early_store(slot, j):
        return pltpu.make_async_copy(
            early_out.at[slot, :, cols(j)], out.at[doc_rows(2 * slot + parity), cols(j)],
            sem_own.at[slot],
        )

    def early_stored(slot):
        return pltpu.make_async_copy(
            early_out.at[slot], out.at[doc_rows(2 * slot + parity)], sem_own.at[slot]
        )

    for j in range(n_chunks):
        x_copy(j).start()
    for n in range(kv_chunks):
        kv_copy(n).start()
    for c in range(SLOTS):
        ring_copy(c).start()

    barrier = pltpu.get_barrier_semaphore()
    pl.semaphore_signal(
        barrier, inc=1, device_id={"tensor": other}, device_id_type=pl.DeviceIdType.MESH
    )
    pl.semaphore_signal(
        barrier, inc=1, device_id={"pipe": following}, device_id_type=pl.DeviceIdType.MESH
    )
    greeted = n_dp + 1
    if n_pipe > 2:
        pl.semaphore_signal(
            barrier, inc=1, device_id={"pipe": preceding}, device_id_type=pl.DeviceIdType.MESH
        )
        greeted += 1
    for away in range(1, n_dp):
        pl.semaphore_signal(
            barrier, inc=1, device_id={"dp": lax.rem(dp + away, n_dp)},
            device_id_type=pl.DeviceIdType.MESH,
        )
    pl.semaphore_wait(barrier, greeted)
    for j in range(n_chunks):
        x_remote(j).start()
    meta_remote().start()

    n_kv = kv_cols.shape[1]
    cols_wide = spread.shape[0]
    out_col = lax.broadcasted_iota(jnp.int32, (128, n_kv), 1)
    wanted = lax.rem(out_col, HD) * KV_HEADS + out_col // HD

    def fill_spread(i, carry):
        base = pl.multiple_of(i * 128, 128)
        row = lax.broadcasted_iota(jnp.int32, (128, n_kv), 0) + base
        spread[pl.ds(base, 128), :] = (row == wanted).astype(jnp.float32).astype(jnp.bfloat16)
        return carry

    lax.fori_loop(0, cols_wide // 128, fill_spread, 0)

    def fill_mask(source):
        row = lax.broadcasted_iota(jnp.int32, (rows, rows), 0)
        col = lax.broadcasted_iota(jnp.int32, (rows, rows), 1)
        row_doc = jnp.zeros((rows, rows), jnp.int32)
        col_doc = jnp.zeros((rows, rows), jnp.int32)
        end = jnp.zeros((1, 1), jnp.int32)
        for d in range(docs):
            end = end + source[0:1, d:d + 1]
            row_doc = row_doc + (row >= end).astype(jnp.int32)
            col_doc = col_doc + (col >= end).astype(jnp.int32)
        allowed = jnp.where((row_doc == col_doc) & (row >= col), 1.0, 0.0)
        for i in range(chunk_heads):
            mask[i * rows:(i + 1) * rows, :] = allowed

    def fill_early_mask():
        row = lax.broadcasted_iota(jnp.int32, (early_rows, early_rows), 0)
        col = lax.broadcasted_iota(jnp.int32, (early_rows, early_rows), 1)
        allowed = jnp.where((row // capacity == col // capacity) & (row >= col), 1.0, 0.0)
        for i in range(chunk_heads):
            early_mask[i * early_rows:(i + 1) * early_rows, :] = allowed

    def fill_valid():
        row = lax.broadcasted_iota(jnp.int32, (capacity, CHUNK), 0)
        for slot in range(half):
            size = jnp.zeros((1, 1), jnp.int32)
            for d in range(docs):
                here = meta_early[slot, 1:2, d:d + 1] == dp
                size = size + jnp.where(here, meta_early[slot, 0:1, d:d + 1], 0)
            valid[slot * capacity:(slot + 1) * capacity, :] = jnp.where(row < size, 1.0, 0.0)

    def fill_choosers(source):
        row = lax.broadcasted_iota(jnp.int32, (1, rows), 1)
        nowhere = jnp.full((1, rows), -1, jnp.int32)
        goals = [nowhere, nowhere]
        begin = jnp.zeros((1, 1), jnp.int32)
        for d in range(docs):
            end = begin + source[0:1, d:d + 1]
            target = source[1:2, d:d + 1]
            place = (target // 2) * capacity + row - begin
            inside = (row >= begin) & (row < end)
            same = target % 2 == parity
            goals = [
                jnp.where(inside & same, place, goals[0]),
                jnp.where(inside & ~same, place, goals[1]),
            ]
            begin = end
        slot = lax.broadcasted_iota(jnp.int32, (early_rows, rows), 0)
        for ref, goal in zip((early_chooser, late_chooser), goals):
            ref[...] = (slot == goal).astype(jnp.float32).astype(jnp.bfloat16)

    def normalise(mine, theirs, first, count):
        held_rows = pl.ds(first, count)

        def squares(j, acc):
            a = mine[j].astype(jnp.float32)
            b = theirs[j].astype(jnp.float32)
            return acc + a * a + b * b

        acc = lax.fori_loop(0, n_chunks, squares, jnp.zeros((count, CHUNK), jnp.float32))
        scale = lax.rsqrt(jnp.sum(acc, axis=-1, keepdims=True) / features + 1e-05)

        def write(j, carry):
            for held, half in ((mine, side), (theirs, other)):
                where = cols(half * n_chunks + j)
                wide = held[j].astype(jnp.float32) * scale * gain[:, where]
                normed[held_rows, where] = wide.astype(jnp.bfloat16)
            return carry

        lax.fori_loop(0, n_chunks, write, 0)

    def keys_values(layer):
        count = layer_rows[layer]

        def one(n, carry):
            if layer == 0:
                kv_copy(n).wait()
            kv_cols[0:count, cols(n)] = jnp.dot(
                normed[0:count, :], kv_weights[n], preferred_element_type=jnp.float32
            ).astype(jnp.bfloat16)
            return carry

        lax.fori_loop(0, kv_chunks, one, 0)
        for which, keep in ((other, False), (side, True)):
            first = pl.multiple_of(which * own_kv * HD, own_kv * HD)
            heads = jnp.dot(
                kv_cols[0:count, :], spread[:, pl.ds(first, own_kv * HD)],
                preferred_element_type=jnp.float32,
            ).astype(jnp.bfloat16)
            for g in range(own_kv):
                if keep:
                    kv_heads[layer, side, g, 0:count] = heads[:, g * HD:(g + 1) * HD]
                else:
                    kv_send[layer, g, 0:count] = heads[:, g * HD:(g + 1) * HD]
            if not keep:
                kv_remote(layer).start()

    def query(layer, c):
        return jnp.dot(
            normed[0:layer_rows[layer], :], ring[lax.rem(c, SLOTS)], preferred_element_type=jnp.float32
        ).astype(jnp.bfloat16)

    def attend(layer, j, mine, first, count, allowed):
        here = slice(first, first + count)
        q = q_held[lax.rem(j, 2), here]
        g = j // group_chunks
        stacked = jnp.concatenate([q[:, i * HD:(i + 1) * HD] for i in range(chunk_heads)], axis=0)
        scores = lax.dot_general(
            stacked, kv_heads[layer, 0, g, here], (((1,), (1,)), ((), ())),
            preferred_element_type=jnp.float32,
        ) * HD ** (-0.5)
        e = jnp.where(allowed[...] > 0.0, jnp.exp(scores), 0.0)
        p = (e * (1.0 / jnp.sum(e, axis=-1, keepdims=True))).astype(jnp.bfloat16)
        a = jnp.dot(p, kv_heads[layer, 1, g, here], preferred_element_type=jnp.float32)
        side_by_side = jnp.concatenate(
            [a[i * count:(i + 1) * count] for i in range(chunk_heads)], axis=1
        )
        return (mine[j].astype(jnp.float32) + side_by_side).astype(jnp.bfloat16)

    def attend_all(layer, j):
        if layer == 0:
            return (attend(0, j, x_own, 0, rows, mask),)
        return (
            attend(1, j, next_own, 0, rows, mask),
            attend(1, j, early_own, rows, early_rows, early_mask),
        )

    def refill(c):
        @pl.when(c + SLOTS < total)
        def _():
            ring_copy(c + SLOTS).start()

    def run_layer(layer, finish):
        count = layer_rows[layer]
        base = layer * n_chunks
        ring_copy(base).wait()
        q_held[0, 0:count] = query(layer, base)
        refill(jnp.int32(base))
        kv_remote(layer).wait()

        def one(j, carry):
            c = base + j
            ring_copy(c).wait()
            fresh = query(layer, c)
            done = attend_all(layer, j - 1)
            q_held[lax.rem(j, 2), 0:count] = fresh
            refill(c)
            finish(j - 1, *done)
            return carry

        lax.fori_loop(1, n_chunks, one, 0)
        finish(n_chunks - 1, *attend_all(layer, n_chunks - 1))

    lag, early_lag = 4, 7

    def pass_on(j):
        h_remote(j).wait_recv()
        forward_remote(j).start()
        picked = jnp.dot(
            early_chooser[...], next_own[j], preferred_element_type=jnp.float32
        ).astype(jnp.bfloat16)
        for slot in range(half):
            early_send[j, slot] = picked[slot * capacity:(slot + 1) * capacity]
        for k in range(1, half):
            early_remote(k, j).start()
        early_own[j, slot_rows(slot_own)] = early_send[j, slot_own]

    def pass_early(j):
        for k in range(1, half):
            early_in(k, j).wait_recv()
        early_forward(j).start()

    def send_next(j, done):
        h_send[j] = done
        h_remote(j).start()

        @pl.when(j >= lag)
        def _():
            pass_on(j - lag)

        @pl.when(j >= early_lag)
        def _():
            pass_early(j - early_lag)

    def send_docs(j, done, early):
        picked = jnp.dot(late_chooser[...], done, preferred_element_type=jnp.float32)
        picked = picked.astype(jnp.bfloat16)
        kept = jnp.where(valid[...] > 0.0, early.astype(jnp.float32), 0.0).astype(jnp.bfloat16)
        for slot in range(half):
            here = slice(slot * capacity, (slot + 1) * capacity)
            packed[slot, :, cols(j)] = picked[here]
            early_out[slot, :, cols(j)] = kept[here]
        for away in range(1, n_dp, 2):
            doc_remote(away, j).start()
        for slot in range(half):
            early_store(slot, j).start()

    fill_mask(meta)
    fill_early_mask()
    meta_remote().wait()
    for k in range(1, half):
        meta_on(k).start()
    meta_early[slot_own] = meta_next[...]
    fill_choosers(meta_next)
    for j in range(n_chunks):
        x_copy(j).wait()
    for j in range(n_chunks):
        x_remote(j).wait()
    normalise(x_own, x_other, 0, rows)
    keys_values(0)
    run_layer(0, send_next)
    for j in range(n_chunks - lag, n_chunks):
        pass_on(j)
    fill_mask(meta_next)
    for k in range(1, half):
        meta_in(k).wait()
    fill_valid()
    for j in range(n_chunks - early_lag, n_chunks):
        pass_early(j)
    for j in range(n_chunks):
        forward_remote(j).wait()
    normalise(next_own, next_other, 0, rows)
    for j in range(n_chunks):
        early_forward(j).wait()
    normalise(early_own, early_other, rows, early_rows)
    keys_values(1)
    run_layer(1, send_docs)
    for j in range(n_chunks):
        h_remote(j).wait_send()
        for k in range(1, half):
            early_remote(k, j).wait_send()
    for slot in range(half):
        early_stored(slot).wait()
    for away in range(1, n_dp, 2):
        doc_all(away).wait()


def fused_device(sizes, hidden, doc_lengths, doc_target, norm_gain, q_weight, kv_weight):
    n_dp, n_pipe, docs = sizes
    rows, width = hidden.shape[1:]
    features = norm_gain.shape[1]
    n_chunks = width // CHUNK
    n_kv = kv_weight.shape[2]
    kv_chunks = n_kv // CHUNK
    own_kv = KV_HEADS // 2
    capacity = rows // 4
    chunk_heads = CHUNK // HD
    meta = jnp.zeros((8, 128), jnp.int32)
    meta = meta.at[0, :docs].set(doc_lengths[0, 0]).at[1, :docs].set(doc_target[0, 0])
    bf16 = jnp.bfloat16
    dma = pltpu.SemaphoreType.DMA
    vmem = pltpu.VMEM
    half = n_dp // 2
    early_rows = half * capacity
    most = rows + early_rows
    blocks = vmem((n_chunks, rows, CHUNK), bf16)
    early_blocks = vmem((n_chunks, early_rows, CHUNK), bf16)
    result = pl.pallas_call(
        functools.partial(fused_kernel, sizes),
        out_shape=jax.ShapeDtypeStruct((n_dp * capacity, width), bf16),
        in_specs=[
            pl.BlockSpec(memory_space=pl.ANY),
            pl.BlockSpec(memory_space=pltpu.VMEM),
            pl.BlockSpec(memory_space=pltpu.VMEM),
            pl.BlockSpec(memory_space=pl.ANY),
            pl.BlockSpec(memory_space=pl.ANY),
        ],
        out_specs=pl.BlockSpec(memory_space=pl.ANY),
        scratch_shapes=[
            blocks, blocks, blocks, blocks, blocks, early_blocks, early_blocks,
            vmem((n_chunks, half, capacity, CHUNK), bf16),
            vmem((8, 128), jnp.int32),
            vmem((half, 8, 128), jnp.int32),
            vmem((most, features), bf16),
            vmem((n_kv, n_kv), bf16),
            vmem((most, n_kv), bf16),
            vmem((STEPS, own_kv, most, HD), bf16),
            vmem((STEPS, 2, own_kv, most, HD), bf16),
            vmem((kv_chunks, features, CHUNK), bf16),
            vmem((SLOTS, features, CHUNK), bf16),
            vmem((chunk_heads * rows, rows), jnp.float32),
            vmem((chunk_heads * early_rows, early_rows), jnp.float32),
            vmem((early_rows, CHUNK), jnp.float32),
            vmem((early_rows, rows), bf16),
            vmem((early_rows, rows), bf16),
            vmem((2, most, CHUNK), bf16),
            vmem((half, capacity, width), bf16),
            vmem((half, capacity, width), bf16),
            dma((n_chunks,)), dma((n_chunks,)), dma((n_chunks,)), dma, dma,
            dma((kv_chunks,)), dma((SLOTS,)), dma((STEPS,)), dma((STEPS,)),
            dma((n_chunks,)), dma((n_chunks,)), dma((n_chunks,)), dma((n_chunks,)),
            dma((n_dp,)), dma((n_dp,)), dma((half,)),
            dma((half, n_chunks)), dma((half, n_chunks)), dma((n_chunks,)), dma((n_chunks,)),
            dma((half,)), dma((half,)),
        ],
        compiler_params=pltpu.CompilerParams(
            collective_id=0, has_side_effects=True, vmem_limit_bytes=67043328
        ),
    )(hidden[0], meta, norm_gain, q_weight[0], kv_weight[0])
    return result[None]


def solution(mesh):
    placed = (
        P("pipe", "dp", "tensor"),
        P("pipe", "dp", None),
        P("pipe", "dp", None),
        P("pipe", None),
        P("pipe", None, "tensor"),
        P("pipe", None, "tensor"),
    )
    run = on_device
    if mesh.shape["tensor"] == 2 and mesh.shape["dp"] % 2 == 0:
        sizes = (mesh.shape["dp"], mesh.shape["pipe"], mesh.shape["dp"])
        run = functools.partial(fused_device, sizes)
    return jax.shard_map(
        run, mesh=mesh, in_specs=placed, out_specs=P("pipe", "dp", "tensor"), check_vma=False
    )
```

```python
import functools

import jax
import jax.numpy as jnp
from jax import lax
from jax.experimental import pallas as pl
from jax.experimental.pallas import tpu as pltpu
from jax.sharding import PartitionSpec as P

D = 8192
HD = 128
KV_HEADS = 8
STEPS = 2


def passed_along(block, axis, distance):
    devices = range(lax.axis_size(axis))
    route = [((i - distance) % len(devices), i) for i in devices]
    return lax.ppermute(block, axis, route)


def build_send(token_rows, lengths, targets, capacity, groups):
    ordinal = jnp.arange(groups, dtype=jnp.int32)
    offsets = jnp.cumsum(lengths) - lengths
    onehot = (targets[None, :] == ordinal[:, None]).astype(jnp.int32)
    doc_sizes = jnp.sum(onehot * lengths[None, :], axis=1)
    doc_starts = jnp.sum(onehot * offsets[None, :], axis=1)
    within = jnp.arange(capacity, dtype=jnp.int32)
    row_index = jnp.minimum(doc_starts[:, None] + within[None, :], token_rows.shape[0] - 1)
    picked = jnp.take(token_rows, row_index.reshape(-1), axis=0).reshape(
        groups, capacity, token_rows.shape[1]
    )
    inside = within[None, :] < doc_sizes[:, None]
    return (jnp.where(inside[:, :, None], picked, jnp.zeros_like(picked)), doc_sizes)


def doc_masks(lengths, length):
    within = jnp.arange(length, dtype=jnp.int32)
    doc_ends = jnp.cumsum(lengths)
    segment = jnp.sum((within[:, None] >= doc_ends[None, :]).astype(jnp.int32), axis=1)
    causal = within[:, None] >= within[None, :]
    return (segment[:, None] == segment[None, :]) & causal


def attend_heads(queries, kv_local, allowed, local_rank):
    row_count = queries.shape[0]
    local_heads = queries.shape[1] // HD
    per_group = D // HD // KV_HEADS
    kv_count = max(1, local_heads // per_group)
    kv_first = local_rank * local_heads // per_group
    kv_whole = lax.all_gather(kv_local, "tensor", axis=1, tiled=True)
    kv_heads = kv_whole.reshape(row_count, 2, HD, KV_HEADS)
    own_heads = lax.dynamic_slice_in_dim(kv_heads, kv_first, kv_count, 3)
    key_rows = own_heads[:, 0]
    values = own_heads[:, 1]
    grouped = queries.reshape(row_count, kv_count, local_heads // kv_count, HD)
    scores = jnp.einsum(
        "qcph,khc->cpqk", grouped, key_rows, preferred_element_type=jnp.float32
    ) * HD ** (-0.5)
    exp_scores = jnp.where(allowed[None, None], jnp.exp(scores), 0.0)
    probabilities = (exp_scores / jnp.sum(exp_scores, axis=-1, keepdims=True)).astype(jnp.bfloat16)
    attended = jnp.einsum(
        "cpqk,khc->qcph", probabilities, values, preferred_element_type=jnp.float32
    )
    return attended.reshape(row_count, queries.shape[1])


def layer_pass(current, gain_full, query_cols, kv_cols, allowed):
    local_rank = lax.axis_index("tensor")
    widened = current.astype(jnp.float32)
    whole = lax.all_gather(current, "tensor", axis=1, tiled=True)
    whole_wide = whole.astype(jnp.float32)
    scale_row = lax.rsqrt(jnp.sum(whole_wide * whole_wide, axis=-1) / D + 1e-05)
    normed_full = (whole_wide * scale_row[:, None] * gain_full).astype(jnp.bfloat16)
    query_sum = jnp.dot(normed_full, query_cols, preferred_element_type=jnp.float32)
    kv_sum = jnp.dot(normed_full, kv_cols, preferred_element_type=jnp.float32)
    queries = query_sum.astype(jnp.bfloat16)
    kv_local = kv_sum.astype(jnp.bfloat16)
    attended = attend_heads(queries, kv_local, allowed, local_rank)
    return (widened + attended).astype(jnp.bfloat16)


def on_device(hidden, doc_lengths, doc_target, norm_gain, q_weight, kv_weight):
    groups = lax.axis_size("dp")
    current = hidden[0]
    lengths = doc_lengths[0, 0]
    targets = doc_target[0, 0]
    capacity = current.shape[0] // 4
    gain_full = norm_gain[0]
    query_cols = q_weight[0]
    kv_cols = kv_weight[0]
    carried = jnp.stack([lengths, targets]).astype(jnp.bfloat16)
    for layer_step in range(STEPS):
        allowed = doc_masks(carried[0].astype(jnp.int32), current.shape[0])
        current = layer_pass(current, gain_full, query_cols, kv_cols, allowed)
        if layer_step + 1 < STEPS:
            current, carried = passed_along((current, carried), "pipe", 1)
    final_lengths = carried[0].astype(jnp.int32)
    final_targets = carried[1].astype(jnp.int32)
    packed, doc_sizes = build_send(current, final_lengths, final_targets, capacity, groups)
    received = lax.all_to_all(packed, "dp", split_axis=0, concat_axis=0, tiled=True)
    return received.reshape(1, groups * capacity, received.shape[2])


CHUNK = 256
SLOTS = 6


def split_masks(n_dp):
    early = [m for m in range(n_dp) if m >= n_dp // 2 and m % 2 == 0]
    return early, [m for m in range(n_dp) if m not in early]


def fused_kernel(
    sizes, hidden, lengths, targets, gain, wq, wkv, out, meta,
    x_own, x_other, h_send, next_own, next_other, early_own, early_other, early_send,
    meta_next, meta_early, normed, spread, kv_cols,
    kv_send, kv_heads, kv_weights, ring, mask, early_mask, valid, early_chooser, late_chooser,
    q_held, packed, early_out,
    sem_x, sem_xs, sem_xr, sem_ms, sem_mr, sem_kvw, sem_ring, sem_kvs, sem_kvr,
    sem_hs, sem_hr, sem_fs, sem_fr, sem_as, sem_ar, sem_own,
    sem_es, sem_er, sem_gs, sem_gr, sem_mes, sem_mer,
):
    n_dp, n_pipe, docs = sizes
    rows, width = hidden.shape
    features = gain.shape[1]
    n_chunks = width // CHUNK
    kv_chunks = wkv.shape[1] // CHUNK
    own_kv = kv_heads.shape[2]
    chunk_heads = CHUNK // HD
    group_chunks = n_chunks // own_kv
    capacity = packed.shape[1]
    early_masks, late_masks = split_masks(n_dp)
    half = len(early_masks)
    early_rows = half * capacity
    dp = lax.axis_index("dp")
    pipe = lax.axis_index("pipe")
    side = lax.axis_index("tensor")
    other = 1 - side
    following = lax.rem(pipe + 1, n_pipe)
    preceding = lax.rem(pipe + n_pipe - 1, n_pipe)
    total = STEPS * n_chunks
    layer_rows = (rows, rows + early_rows)

    def partner(flips):
        index, bit = dp, 1
        while bit < n_dp:
            if flips & bit:
                index = index + bit - 2 * bit * lax.rem(dp // bit, 2)
            bit *= 2
        return index

    early_partners = [partner(m) for m in early_masks]
    late_partners = [partner(m) for m in late_masks]

    def cols(j):
        return pl.ds(pl.multiple_of(j * CHUNK, CHUNK), CHUNK)

    def kv_copy(n):
        return pltpu.make_async_copy(wkv.at[:, cols(n)], kv_weights.at[n], sem_kvw.at[n])

    def ring_copy(c):
        slot = lax.rem(c, SLOTS)
        return pltpu.make_async_copy(
            wq.at[:, cols(lax.rem(c, n_chunks))], ring.at[slot], sem_ring.at[slot]
        )

    def x_copy(j):
        return pltpu.make_async_copy(hidden.at[:, cols(j)], x_own.at[j], sem_x.at[j])

    def x_remote(j):
        return pltpu.make_async_remote_copy(
            hidden.at[:, cols(j)], x_other.at[j], sem_xs.at[j], sem_xr.at[j],
            device_id={"tensor": other}, device_id_type=pl.DeviceIdType.MESH,
        )

    def meta_remote():
        return pltpu.make_async_remote_copy(
            meta, meta_next, sem_ms, sem_mr,
            device_id={"pipe": following}, device_id_type=pl.DeviceIdType.MESH,
        )

    def meta_on(k):
        return pltpu.make_async_remote_copy(
            meta_next, meta_early.at[k], sem_mes.at[k], sem_mer.at[k],
            device_id={"dp": early_partners[k]}, device_id_type=pl.DeviceIdType.MESH,
        )

    def early_remote(k, j):
        return pltpu.make_async_remote_copy(
            early_send.at[j, k], early_own.at[j, k * capacity:(k + 1) * capacity],
            sem_es.at[k, j], sem_er.at[k, j],
            device_id={"dp": early_partners[k]}, device_id_type=pl.DeviceIdType.MESH,
        )

    def early_forward(j):
        return pltpu.make_async_remote_copy(
            early_own.at[j], early_other.at[j], sem_gs.at[j], sem_gr.at[j],
            device_id={"tensor": other}, device_id_type=pl.DeviceIdType.MESH,
        )

    def kv_remote(layer):
        here = pl.ds(0, layer_rows[layer])
        return pltpu.make_async_remote_copy(
            kv_send.at[layer, :, here], kv_heads.at[layer, side, :, here], sem_kvs.at[layer], sem_kvr.at[layer],
            device_id={"tensor": other}, device_id_type=pl.DeviceIdType.MESH,
        )

    def h_remote(j):
        return pltpu.make_async_remote_copy(
            h_send.at[j], next_own.at[j], sem_hs.at[j], sem_hr.at[j],
            device_id={"pipe": following}, device_id_type=pl.DeviceIdType.MESH,
        )

    def forward_remote(j):
        return pltpu.make_async_remote_copy(
            next_own.at[j], next_other.at[j], sem_fs.at[j], sem_fr.at[j],
            device_id={"tensor": other}, device_id_type=pl.DeviceIdType.MESH,
        )

    def doc_rows(index):
        return pl.ds(pl.multiple_of(index * capacity, capacity), capacity)

    def doc_remote(k, j):
        return pltpu.make_async_remote_copy(
            packed.at[k, :, cols(j)], out.at[doc_rows(dp), cols(j)],
            sem_as.at[k], sem_ar.at[k],
            device_id={"dp": late_partners[k]}, device_id_type=pl.DeviceIdType.MESH,
        )

    def doc_all(k):
        return pltpu.make_async_remote_copy(
            packed.at[k], out.at[doc_rows(late_partners[k])],
            sem_as.at[k], sem_ar.at[k],
            device_id={"dp": late_partners[k]}, device_id_type=pl.DeviceIdType.MESH,
        )

    def own_store(j):
        return pltpu.make_async_copy(
            packed.at[0, :, cols(j)], out.at[doc_rows(dp), cols(j)], sem_own.at[half]
        )

    def own_stored():
        return pltpu.make_async_copy(packed.at[0], out.at[doc_rows(dp)], sem_own.at[half])

    def early_store(k, j):
        return pltpu.make_async_copy(
            early_out.at[k, :, cols(j)], out.at[doc_rows(early_partners[k]), cols(j)],
            sem_own.at[k],
        )

    def early_stored(k):
        return pltpu.make_async_copy(
            early_out.at[k], out.at[doc_rows(early_partners[k])], sem_own.at[k]
        )

    for j in range(n_chunks):
        x_copy(j).start()
    for n in range(kv_chunks):
        kv_copy(n).start()
    for c in range(SLOTS):
        ring_copy(c).start()

    meta[...] = jnp.zeros(meta.shape, jnp.int32)
    meta[0:1, 0:docs] = lengths[...]
    meta[1:2, 0:docs] = targets[...]
    barrier = pltpu.get_barrier_semaphore()
    pl.semaphore_signal(
        barrier, inc=1, device_id={"tensor": other}, device_id_type=pl.DeviceIdType.MESH
    )
    pl.semaphore_signal(
        barrier, inc=1, device_id={"pipe": following}, device_id_type=pl.DeviceIdType.MESH
    )
    greeted = n_dp + 1
    if n_pipe > 2:
        pl.semaphore_signal(
            barrier, inc=1, device_id={"pipe": preceding}, device_id_type=pl.DeviceIdType.MESH
        )
        greeted += 1
    for away in range(1, n_dp):
        pl.semaphore_signal(
            barrier, inc=1, device_id={"dp": lax.rem(dp + away, n_dp)},
            device_id_type=pl.DeviceIdType.MESH,
        )
    pl.semaphore_wait(barrier, greeted)
    for j in range(n_chunks):
        x_remote(j).start()
    meta_remote().start()

    n_kv = kv_cols.shape[1]
    cols_wide = spread.shape[0]
    out_col = lax.broadcasted_iota(jnp.int32, (128, n_kv), 1)
    wanted = lax.rem(out_col, HD) * KV_HEADS + out_col // HD

    def fill_spread(i, carry):
        base = pl.multiple_of(i * 128, 128)
        row = lax.broadcasted_iota(jnp.int32, (128, n_kv), 0) + base
        spread[pl.ds(base, 128), :] = (row == wanted).astype(jnp.float32).astype(jnp.bfloat16)
        return carry

    lax.fori_loop(0, cols_wide // 128, fill_spread, 0)

    def fill_mask(source):
        row = lax.broadcasted_iota(jnp.int32, (rows, rows), 0)
        col = lax.broadcasted_iota(jnp.int32, (rows, rows), 1)
        row_doc = jnp.zeros((rows, rows), jnp.int32)
        col_doc = jnp.zeros((rows, rows), jnp.int32)
        end = jnp.zeros((1, 1), jnp.int32)
        for d in range(docs):
            end = end + source[0:1, d:d + 1]
            row_doc = row_doc + (row >= end).astype(jnp.int32)
            col_doc = col_doc + (col >= end).astype(jnp.int32)
        allowed = jnp.where((row_doc == col_doc) & (row >= col), 1.0, 0.0)
        for i in range(chunk_heads):
            mask[i * rows:(i + 1) * rows, :] = allowed

    def fill_early_mask():
        row = lax.broadcasted_iota(jnp.int32, (early_rows, early_rows), 0)
        col = lax.broadcasted_iota(jnp.int32, (early_rows, early_rows), 1)
        allowed = jnp.where((row // capacity == col // capacity) & (row >= col), 1.0, 0.0)
        for i in range(chunk_heads):
            early_mask[i * early_rows:(i + 1) * early_rows, :] = allowed

    def fill_valid():
        row = lax.broadcasted_iota(jnp.int32, (capacity, CHUNK), 0)
        for slot in range(half):
            size = jnp.zeros((1, 1), jnp.int32)
            for d in range(docs):
                here = meta_early[slot, 1:2, d:d + 1] == dp
                size = size + jnp.where(here, meta_early[slot, 0:1, d:d + 1], 0)
            valid[slot * capacity:(slot + 1) * capacity, :] = jnp.where(row < size, 1.0, 0.0)

    def fill_choosers(source):
        row = lax.broadcasted_iota(jnp.int32, (1, rows), 1)
        goals = [jnp.full((1, rows), -1, jnp.int32) for _ in range(2)]
        begin = jnp.zeros((1, 1), jnp.int32)
        for d in range(docs):
            end = begin + source[0:1, d:d + 1]
            target = source[1:2, d:d + 1]
            inside = (row >= begin) & (row < end)
            for i, partners in enumerate((early_partners, late_partners)):
                first = jnp.full((1, 1), -n_dp * capacity, jnp.int32)
                for k, index in enumerate(partners):
                    first = jnp.where(target == index, k * capacity, first)
                goals[i] = jnp.where(inside, first + row - begin, goals[i])
            begin = end
        for ref, goal in zip((early_chooser, late_chooser), goals):
            slot = lax.broadcasted_iota(jnp.int32, ref.shape, 0)
            ref[...] = (slot == goal).astype(jnp.float32).astype(jnp.bfloat16)

    def normalise(mine, theirs, first, count):
        held_rows = pl.ds(first, count)

        def squares(j, acc):
            a = mine[j].astype(jnp.float32)
            b = theirs[j].astype(jnp.float32)
            return acc + a * a + b * b

        acc = lax.fori_loop(0, n_chunks, squares, jnp.zeros((count, CHUNK), jnp.float32))
        scale = lax.rsqrt(jnp.sum(acc, axis=-1, keepdims=True) / features + 1e-05)

        def write(j, carry):
            for held, half in ((mine, side), (theirs, other)):
                where = cols(half * n_chunks + j)
                wide = held[j].astype(jnp.float32) * scale * gain[:, where]
                normed[held_rows, where] = wide.astype(jnp.bfloat16)
            return carry

        lax.fori_loop(0, n_chunks, write, 0)

    def keys_values(layer):
        count = layer_rows[layer]

        def one(n, carry):
            if layer == 0:
                kv_copy(n).wait()
            kv_cols[0:count, cols(n)] = jnp.dot(
                normed[0:count, :], kv_weights[n], preferred_element_type=jnp.float32
            ).astype(jnp.bfloat16)
            return carry

        lax.fori_loop(0, kv_chunks, one, 0)
        for which, keep in ((other, False), (side, True)):
            first = pl.multiple_of(which * own_kv * HD, own_kv * HD)
            heads = jnp.dot(
                kv_cols[0:count, :], spread[:, pl.ds(first, own_kv * HD)],
                preferred_element_type=jnp.float32,
            ).astype(jnp.bfloat16)
            for g in range(own_kv):
                if keep:
                    kv_heads[layer, side, g, 0:count] = heads[:, g * HD:(g + 1) * HD]
                else:
                    kv_send[layer, g, 0:count] = heads[:, g * HD:(g + 1) * HD]
            if not keep:
                kv_remote(layer).start()

    def query(layer, c):
        return jnp.dot(
            normed[0:layer_rows[layer], :], ring[lax.rem(c, SLOTS)], preferred_element_type=jnp.float32
        ).astype(jnp.bfloat16)

    def attend(layer, j, mine, first, count, allowed):
        here = slice(first, first + count)
        q = q_held[lax.rem(j, 2), here]
        g = j // group_chunks
        stacked = jnp.concatenate([q[:, i * HD:(i + 1) * HD] for i in range(chunk_heads)], axis=0)
        scores = lax.dot_general(
            stacked, kv_heads[layer, 0, g, here], (((1,), (1,)), ((), ())),
            preferred_element_type=jnp.float32,
        ) * HD ** (-0.5)
        e = jnp.where(allowed[...] > 0.0, jnp.exp(scores), 0.0)
        p = (e * (1.0 / jnp.sum(e, axis=-1, keepdims=True))).astype(jnp.bfloat16)
        a = jnp.dot(p, kv_heads[layer, 1, g, here], preferred_element_type=jnp.float32)
        side_by_side = jnp.concatenate(
            [a[i * count:(i + 1) * count] for i in range(chunk_heads)], axis=1
        )
        return (mine[j].astype(jnp.float32) + side_by_side).astype(jnp.bfloat16)

    def attend_all(layer, j):
        if layer == 0:
            return (attend(0, j, x_own, 0, rows, mask),)
        return (
            attend(1, j, next_own, 0, rows, mask),
            attend(1, j, early_own, rows, early_rows, early_mask),
        )

    def refill(c):
        @pl.when(c + SLOTS < total)
        def _():
            ring_copy(c + SLOTS).start()

    def run_layer(layer, finish):
        count = layer_rows[layer]
        base = layer * n_chunks
        ring_copy(base).wait()
        q_held[0, 0:count] = query(layer, base)
        refill(jnp.int32(base))
        kv_remote(layer).wait()

        def one(j, carry):
            c = base + j
            ring_copy(c).wait()
            fresh = query(layer, c)
            done = attend_all(layer, j - 1)
            q_held[lax.rem(j, 2), 0:count] = fresh
            refill(c)
            finish(j - 1, *done)
            return carry

        lax.fori_loop(1, n_chunks, one, 0)
        finish(n_chunks - 1, *attend_all(layer, n_chunks - 1))

    lag, early_lag = 4, 7

    def pass_on(j):
        h_remote(j).wait_recv()
        forward_remote(j).start()
        picked = jnp.dot(
            early_chooser[...], next_own[j], preferred_element_type=jnp.float32
        ).astype(jnp.bfloat16)
        for slot in range(half):
            early_send[j, slot] = picked[slot * capacity:(slot + 1) * capacity]
        for k in range(half):
            early_remote(k, j).start()

    def pass_early(j):
        for k in range(half):
            early_remote(k, j).wait_recv()
        early_forward(j).start()

    def send_next(j, done):
        h_send[j] = done
        h_remote(j).start()

        @pl.when(j >= lag)
        def _():
            pass_on(j - lag)

        @pl.when(j >= early_lag)
        def _():
            pass_early(j - early_lag)

    def send_docs(j, done, early):
        picked = jnp.dot(late_chooser[...], done, preferred_element_type=jnp.float32)
        picked = picked.astype(jnp.bfloat16)
        kept = jnp.where(valid[...] > 0.0, early.astype(jnp.float32), 0.0).astype(jnp.bfloat16)
        for slot in range(len(late_masks)):
            packed[slot, :, cols(j)] = picked[slot * capacity:(slot + 1) * capacity]
        for k in reversed(range(1, len(late_masks))):
            doc_remote(k, j).start()
        own_store(j).start()
        for slot in range(half):
            early_out[slot, :, cols(j)] = kept[slot * capacity:(slot + 1) * capacity]
        for slot in range(half):
            early_store(slot, j).start()

    fill_mask(meta)
    fill_early_mask()
    meta_remote().wait()
    for k in range(half):
        meta_on(k).start()
    fill_choosers(meta_next)
    for j in range(n_chunks):
        x_copy(j).wait()
    for j in range(n_chunks):
        x_remote(j).wait()
    normalise(x_own, x_other, 0, rows)
    keys_values(0)
    run_layer(0, send_next)
    for j in range(n_chunks - lag, n_chunks):
        pass_on(j)
    fill_mask(meta_next)
    for k in range(half):
        meta_on(k).wait()
    fill_valid()
    for j in range(n_chunks - early_lag, n_chunks):
        pass_early(j)
    for j in range(n_chunks):
        forward_remote(j).wait()
    normalise(next_own, next_other, 0, rows)
    for j in range(n_chunks):
        early_forward(j).wait()
    normalise(early_own, early_other, rows, early_rows)
    keys_values(1)
    run_layer(1, send_docs)
    for j in range(n_chunks):
        h_remote(j).wait_send()
        for k in range(half):
            early_remote(k, j).wait_send()
    for slot in range(half):
        early_stored(slot).wait()
    own_stored().wait()
    for k in range(1, len(late_masks)):
        doc_all(k).wait()


def fused_device(sizes, hidden, doc_lengths, doc_target, norm_gain, q_weight, kv_weight):
    n_dp, n_pipe, docs = sizes
    rows, width = hidden.shape[1:]
    features = norm_gain.shape[1]
    n_chunks = width // CHUNK
    n_kv = kv_weight.shape[2]
    kv_chunks = n_kv // CHUNK
    own_kv = KV_HEADS // 2
    capacity = rows // 4
    chunk_heads = CHUNK // HD
    bf16 = jnp.bfloat16
    dma = pltpu.SemaphoreType.DMA
    vmem = pltpu.VMEM
    early_masks, late_masks = split_masks(n_dp)
    half, n_late = len(early_masks), len(late_masks)
    early_rows = half * capacity
    most = rows + early_rows
    blocks = vmem((n_chunks, rows, CHUNK), bf16)
    early_blocks = vmem((n_chunks, early_rows, CHUNK), bf16)
    result = pl.pallas_call(
        functools.partial(fused_kernel, sizes),
        out_shape=jax.ShapeDtypeStruct((n_dp * capacity, width), bf16),
        in_specs=[
            pl.BlockSpec(memory_space=pl.ANY),
            pl.BlockSpec(memory_space=pltpu.VMEM),
            pl.BlockSpec(memory_space=pltpu.VMEM),
            pl.BlockSpec(memory_space=pltpu.VMEM),
            pl.BlockSpec(memory_space=pl.ANY),
            pl.BlockSpec(memory_space=pl.ANY),
        ],
        out_specs=pl.BlockSpec(memory_space=pl.ANY),
        scratch_shapes=[
            vmem((8, 128), jnp.int32),
            blocks, blocks, blocks, blocks, blocks, early_blocks, early_blocks,
            vmem((n_chunks, half, capacity, CHUNK), bf16),
            vmem((8, 128), jnp.int32),
            vmem((half, 8, 128), jnp.int32),
            vmem((most, features), bf16),
            vmem((n_kv, n_kv), bf16),
            vmem((most, n_kv), bf16),
            vmem((STEPS, own_kv, most, HD), bf16),
            vmem((STEPS, 2, own_kv, most, HD), bf16),
            vmem((kv_chunks, features, CHUNK), bf16),
            vmem((SLOTS, features, CHUNK), bf16),
            vmem((chunk_heads * rows, rows), jnp.float32),
            vmem((chunk_heads * early_rows, early_rows), jnp.float32),
            vmem((early_rows, CHUNK), jnp.float32),
            vmem((early_rows, rows), bf16),
            vmem((n_late * capacity, rows), bf16),
            vmem((2, most, CHUNK), bf16),
            vmem((n_late, capacity, width), bf16),
            vmem((half, capacity, width), bf16),
            dma((n_chunks,)), dma((n_chunks,)), dma((n_chunks,)), dma, dma,
            dma((kv_chunks,)), dma((SLOTS,)), dma((STEPS,)), dma((STEPS,)),
            dma((n_chunks,)), dma((n_chunks,)), dma((n_chunks,)), dma((n_chunks,)),
            dma((n_late,)), dma((n_late,)), dma((half + 1,)),
            dma((half, n_chunks)), dma((half, n_chunks)), dma((n_chunks,)), dma((n_chunks,)),
            dma((half,)), dma((half,)),
        ],
        compiler_params=pltpu.CompilerParams(
            collective_id=0, has_side_effects=True, vmem_limit_bytes=67043328
        ),
    )(hidden[0], doc_lengths[0], doc_target[0], norm_gain, q_weight[0], kv_weight[0])
    return result[None]


def solution(mesh):
    placed = (
        P("pipe", "dp", "tensor"),
        P("pipe", "dp", None),
        P("pipe", "dp", None),
        P("pipe", None),
        P("pipe", None, "tensor"),
        P("pipe", None, "tensor"),
    )
    run = on_device
    if mesh.shape["tensor"] == 2 and mesh.shape["dp"] in (4, 8, 16):
        sizes = (mesh.shape["dp"], mesh.shape["pipe"], mesh.shape["dp"])
        run = functools.partial(fused_device, sizes)
    return jax.shard_map(
        run, mesh=mesh, in_specs=placed, out_specs=P("pipe", "dp", "tensor"), check_vma=False
    )
```

```python
import functools

import jax
import jax.numpy as jnp
from jax import lax
from jax.experimental import pallas as pl
from jax.experimental.pallas import tpu as pltpu
from jax.sharding import PartitionSpec as P

D = 8192
HD = 128
KV_HEADS = 8
STEPS = 2


def passed_along(block, axis, distance):
    devices = range(lax.axis_size(axis))
    route = [((i - distance) % len(devices), i) for i in devices]
    return lax.ppermute(block, axis, route)


def build_send(token_rows, lengths, targets, capacity, groups):
    ordinal = jnp.arange(groups, dtype=jnp.int32)
    offsets = jnp.cumsum(lengths) - lengths
    onehot = (targets[None, :] == ordinal[:, None]).astype(jnp.int32)
    doc_sizes = jnp.sum(onehot * lengths[None, :], axis=1)
    doc_starts = jnp.sum(onehot * offsets[None, :], axis=1)
    within = jnp.arange(capacity, dtype=jnp.int32)
    row_index = jnp.minimum(doc_starts[:, None] + within[None, :], token_rows.shape[0] - 1)
    picked = jnp.take(token_rows, row_index.reshape(-1), axis=0).reshape(
        groups, capacity, token_rows.shape[1]
    )
    inside = within[None, :] < doc_sizes[:, None]
    return (jnp.where(inside[:, :, None], picked, jnp.zeros_like(picked)), doc_sizes)


def doc_masks(lengths, length):
    within = jnp.arange(length, dtype=jnp.int32)
    doc_ends = jnp.cumsum(lengths)
    segment = jnp.sum((within[:, None] >= doc_ends[None, :]).astype(jnp.int32), axis=1)
    causal = within[:, None] >= within[None, :]
    return (segment[:, None] == segment[None, :]) & causal


def attend_heads(queries, kv_local, allowed, local_rank):
    row_count = queries.shape[0]
    local_heads = queries.shape[1] // HD
    per_group = D // HD // KV_HEADS
    kv_count = max(1, local_heads // per_group)
    kv_first = local_rank * local_heads // per_group
    kv_whole = lax.all_gather(kv_local, "tensor", axis=1, tiled=True)
    kv_heads = kv_whole.reshape(row_count, 2, HD, KV_HEADS)
    own_heads = lax.dynamic_slice_in_dim(kv_heads, kv_first, kv_count, 3)
    key_rows = own_heads[:, 0]
    values = own_heads[:, 1]
    grouped = queries.reshape(row_count, kv_count, local_heads // kv_count, HD)
    scores = jnp.einsum(
        "qcph,khc->cpqk", grouped, key_rows, preferred_element_type=jnp.float32
    ) * HD ** (-0.5)
    exp_scores = jnp.where(allowed[None, None], jnp.exp(scores), 0.0)
    probabilities = (exp_scores / jnp.sum(exp_scores, axis=-1, keepdims=True)).astype(jnp.bfloat16)
    attended = jnp.einsum(
        "cpqk,khc->qcph", probabilities, values, preferred_element_type=jnp.float32
    )
    return attended.reshape(row_count, queries.shape[1])


def layer_pass(current, gain_full, query_cols, kv_cols, allowed):
    local_rank = lax.axis_index("tensor")
    widened = current.astype(jnp.float32)
    whole = lax.all_gather(current, "tensor", axis=1, tiled=True)
    whole_wide = whole.astype(jnp.float32)
    scale_row = lax.rsqrt(jnp.sum(whole_wide * whole_wide, axis=-1) / D + 1e-05)
    normed_full = (whole_wide * scale_row[:, None] * gain_full).astype(jnp.bfloat16)
    query_sum = jnp.dot(normed_full, query_cols, preferred_element_type=jnp.float32)
    kv_sum = jnp.dot(normed_full, kv_cols, preferred_element_type=jnp.float32)
    queries = query_sum.astype(jnp.bfloat16)
    kv_local = kv_sum.astype(jnp.bfloat16)
    attended = attend_heads(queries, kv_local, allowed, local_rank)
    return (widened + attended).astype(jnp.bfloat16)


def on_device(hidden, doc_lengths, doc_target, norm_gain, q_weight, kv_weight):
    groups = lax.axis_size("dp")
    current = hidden[0]
    lengths = doc_lengths[0, 0]
    targets = doc_target[0, 0]
    capacity = current.shape[0] // 4
    gain_full = norm_gain[0]
    query_cols = q_weight[0]
    kv_cols = kv_weight[0]
    carried = jnp.stack([lengths, targets]).astype(jnp.bfloat16)
    for layer_step in range(STEPS):
        allowed = doc_masks(carried[0].astype(jnp.int32), current.shape[0])
        current = layer_pass(current, gain_full, query_cols, kv_cols, allowed)
        if layer_step + 1 < STEPS:
            current, carried = passed_along((current, carried), "pipe", 1)
    final_lengths = carried[0].astype(jnp.int32)
    final_targets = carried[1].astype(jnp.int32)
    packed, doc_sizes = build_send(current, final_lengths, final_targets, capacity, groups)
    received = lax.all_to_all(packed, "dp", split_axis=0, concat_axis=0, tiled=True)
    return received.reshape(1, groups * capacity, received.shape[2])


CHUNK = 256
SLOTS = 6


def split_masks(n_dp):
    early = [m for m in range(n_dp) if m >= n_dp // 2 and m % 2 == 0]
    return early, [m for m in range(n_dp) if m not in early]


def fused_kernel(
    sizes, hidden, lengths, targets, gain, wq, wkv, out, meta,
    x_own, x_other, h_send, next_own, next_other, early_own, early_other, early_send,
    meta_next, meta_early, normed, spread, kv_cols,
    kv_send, kv_heads, kv_weights, ring, mask, early_mask, valid, early_chooser, late_chooser,
    q_held, packed, early_out,
    sem_x, sem_xs, sem_xr, sem_ms, sem_mr, sem_kvw, sem_ring, sem_kvs, sem_kvr,
    sem_hs, sem_hr, sem_fs, sem_fr, sem_as, sem_ar, sem_own,
    sem_es, sem_er, sem_gs, sem_gr, sem_mes, sem_mer,
):
    n_dp, n_pipe, docs = sizes
    rows, width = hidden.shape
    features = gain.shape[1]
    n_chunks = width // CHUNK
    kv_chunks = wkv.shape[1] // CHUNK
    own_kv = kv_heads.shape[2]
    chunk_heads = CHUNK // HD
    group_chunks = n_chunks // own_kv
    capacity = packed.shape[1]
    early_masks, late_masks = split_masks(n_dp)
    half = len(early_masks)
    early_rows = half * capacity
    dp = lax.axis_index("dp")
    pipe = lax.axis_index("pipe")
    side = lax.axis_index("tensor")
    other = 1 - side
    following = lax.rem(pipe + 1, n_pipe)
    preceding = lax.rem(pipe + n_pipe - 1, n_pipe)
    total = STEPS * n_chunks
    layer_rows = (rows, rows + early_rows)

    def partner(flips):
        index, bit = dp, 1
        while bit < n_dp:
            if flips & bit:
                index = index + bit - 2 * bit * lax.rem(dp // bit, 2)
            bit *= 2
        return index

    early_partners = [partner(m) for m in early_masks]
    late_partners = [partner(m) for m in late_masks]

    def cols(j):
        return pl.ds(pl.multiple_of(j * CHUNK, CHUNK), CHUNK)

    def kv_copy(n):
        return pltpu.make_async_copy(wkv.at[:, cols(n)], kv_weights.at[n], sem_kvw.at[n])

    def ring_copy(c):
        slot = lax.rem(c, SLOTS)
        return pltpu.make_async_copy(
            wq.at[:, cols(lax.rem(c, n_chunks))], ring.at[slot], sem_ring.at[slot]
        )

    def x_copy(j):
        return pltpu.make_async_copy(hidden.at[:, cols(j)], x_own.at[j], sem_x.at[j])

    def x_remote(j):
        return pltpu.make_async_remote_copy(
            x_own.at[j], x_other.at[j], sem_xs.at[j], sem_xr.at[j],
            device_id={"tensor": other}, device_id_type=pl.DeviceIdType.MESH,
        )

    def meta_remote():
        return pltpu.make_async_remote_copy(
            meta, meta_next, sem_ms, sem_mr,
            device_id={"pipe": following}, device_id_type=pl.DeviceIdType.MESH,
        )

    def meta_on(k):
        return pltpu.make_async_remote_copy(
            meta_next, meta_early.at[k], sem_mes.at[k], sem_mer.at[k],
            device_id={"dp": early_partners[k]}, device_id_type=pl.DeviceIdType.MESH,
        )

    def early_remote(k, j):
        return pltpu.make_async_remote_copy(
            early_send.at[j, k], early_own.at[j, k * capacity:(k + 1) * capacity],
            sem_es.at[k, j], sem_er.at[k, j],
            device_id={"dp": early_partners[k]}, device_id_type=pl.DeviceIdType.MESH,
        )

    def early_forward(j):
        return pltpu.make_async_remote_copy(
            early_own.at[j], early_other.at[j], sem_gs.at[j], sem_gr.at[j],
            device_id={"tensor": other}, device_id_type=pl.DeviceIdType.MESH,
        )

    def kv_remote(layer):
        here = pl.ds(0, layer_rows[layer])
        return pltpu.make_async_remote_copy(
            kv_send.at[layer, :, here], kv_heads.at[layer, side, :, here], sem_kvs.at[layer], sem_kvr.at[layer],
            device_id={"tensor": other}, device_id_type=pl.DeviceIdType.MESH,
        )

    def h_remote(j):
        return pltpu.make_async_remote_copy(
            h_send.at[j], next_own.at[j], sem_hs.at[j], sem_hr.at[j],
            device_id={"pipe": following}, device_id_type=pl.DeviceIdType.MESH,
        )

    def forward_remote(j):
        return pltpu.make_async_remote_copy(
            next_own.at[j], next_other.at[j], sem_fs.at[j], sem_fr.at[j],
            device_id={"tensor": other}, device_id_type=pl.DeviceIdType.MESH,
        )

    def doc_rows(index):
        return pl.ds(pl.multiple_of(index * capacity, capacity), capacity)

    def doc_remote(k, j):
        return pltpu.make_async_remote_copy(
            packed.at[k, :, cols(j)], out.at[doc_rows(dp), cols(j)],
            sem_as.at[k], sem_ar.at[k],
            device_id={"dp": late_partners[k]}, device_id_type=pl.DeviceIdType.MESH,
        )

    def doc_all(k):
        return pltpu.make_async_remote_copy(
            packed.at[k], out.at[doc_rows(late_partners[k])],
            sem_as.at[k], sem_ar.at[k],
            device_id={"dp": late_partners[k]}, device_id_type=pl.DeviceIdType.MESH,
        )

    def own_store(j):
        return pltpu.make_async_copy(
            packed.at[0, :, cols(j)], out.at[doc_rows(dp), cols(j)], sem_own.at[half]
        )

    def own_stored():
        return pltpu.make_async_copy(packed.at[0], out.at[doc_rows(dp)], sem_own.at[half])

    def early_store(k, j):
        return pltpu.make_async_copy(
            early_out.at[k, :, cols(j)], out.at[doc_rows(early_partners[k]), cols(j)],
            sem_own.at[k],
        )

    def early_stored(k):
        return pltpu.make_async_copy(
            early_out.at[k], out.at[doc_rows(early_partners[k])], sem_own.at[k]
        )

    for j in range(n_chunks):
        x_copy(j).start()
    for n in range(kv_chunks):
        kv_copy(n).start()
    for c in range(SLOTS):
        ring_copy(c).start()

    meta[...] = jnp.zeros(meta.shape, jnp.int32)
    meta[0:1, 0:docs] = lengths[...]
    meta[1:2, 0:docs] = targets[...]
    barrier = pltpu.get_barrier_semaphore()
    pl.semaphore_signal(
        barrier, inc=1, device_id={"tensor": other}, device_id_type=pl.DeviceIdType.MESH
    )
    pl.semaphore_signal(
        barrier, inc=1, device_id={"pipe": following}, device_id_type=pl.DeviceIdType.MESH
    )
    greeted = n_dp + 1
    if n_pipe > 2:
        pl.semaphore_signal(
            barrier, inc=1, device_id={"pipe": preceding}, device_id_type=pl.DeviceIdType.MESH
        )
        greeted += 1
    for away in range(1, n_dp):
        pl.semaphore_signal(
            barrier, inc=1, device_id={"dp": lax.rem(dp + away, n_dp)},
            device_id_type=pl.DeviceIdType.MESH,
        )
    pl.semaphore_wait(barrier, greeted)
    meta_remote().start()
    for j in range(n_chunks):
        x_copy(j).wait()
        x_remote(j).start()

    n_kv = kv_cols.shape[1]
    cols_wide = spread.shape[0]
    out_col = lax.broadcasted_iota(jnp.int32, (128, n_kv), 1)
    wanted = lax.rem(out_col, HD) * KV_HEADS + out_col // HD

    def fill_spread(i, carry):
        base = pl.multiple_of(i * 128, 128)
        row = lax.broadcasted_iota(jnp.int32, (128, n_kv), 0) + base
        spread[pl.ds(base, 128), :] = (row == wanted).astype(jnp.float32).astype(jnp.bfloat16)
        return carry

    lax.fori_loop(0, cols_wide // 128, fill_spread, 0)

    def fill_mask(source):
        row = lax.broadcasted_iota(jnp.int32, (rows, rows), 0)
        col = lax.broadcasted_iota(jnp.int32, (rows, rows), 1)
        row_doc = jnp.zeros((rows, rows), jnp.int32)
        col_doc = jnp.zeros((rows, rows), jnp.int32)
        end = jnp.zeros((1, 1), jnp.int32)
        for d in range(docs):
            end = end + source[0:1, d:d + 1]
            row_doc = row_doc + (row >= end).astype(jnp.int32)
            col_doc = col_doc + (col >= end).astype(jnp.int32)
        allowed = jnp.where((row_doc == col_doc) & (row >= col), 1.0, 0.0)
        for i in range(chunk_heads):
            mask[i * rows:(i + 1) * rows, :] = allowed

    def fill_early_mask():
        row = lax.broadcasted_iota(jnp.int32, (early_rows, early_rows), 0)
        col = lax.broadcasted_iota(jnp.int32, (early_rows, early_rows), 1)
        allowed = jnp.where((row // capacity == col // capacity) & (row >= col), 1.0, 0.0)
        for i in range(chunk_heads):
            early_mask[i * early_rows:(i + 1) * early_rows, :] = allowed

    def fill_valid():
        row = lax.broadcasted_iota(jnp.int32, (capacity, CHUNK), 0)
        for slot in range(half):
            size = jnp.zeros((1, 1), jnp.int32)
            for d in range(docs):
                here = meta_early[slot, 1:2, d:d + 1] == dp
                size = size + jnp.where(here, meta_early[slot, 0:1, d:d + 1], 0)
            valid[slot * capacity:(slot + 1) * capacity, :] = jnp.where(row < size, 1.0, 0.0)

    def fill_choosers(source):
        row = lax.broadcasted_iota(jnp.int32, (1, rows), 1)
        goals = [jnp.full((1, rows), -1, jnp.int32) for _ in range(2)]
        begin = jnp.zeros((1, 1), jnp.int32)
        for d in range(docs):
            end = begin + source[0:1, d:d + 1]
            target = source[1:2, d:d + 1]
            inside = (row >= begin) & (row < end)
            for i, partners in enumerate((early_partners, late_partners)):
                first = jnp.full((1, 1), -n_dp * capacity, jnp.int32)
                for k, index in enumerate(partners):
                    first = jnp.where(target == index, k * capacity, first)
                goals[i] = jnp.where(inside, first + row - begin, goals[i])
            begin = end
        for ref, goal in zip((early_chooser, late_chooser), goals):
            slot = lax.broadcasted_iota(jnp.int32, ref.shape, 0)
            ref[...] = (slot == goal).astype(jnp.float32).astype(jnp.bfloat16)

    def normalise(mine, theirs, first, count):
        held_rows = pl.ds(first, count)

        def squares(j, acc):
            a = mine[j].astype(jnp.float32)
            b = theirs[j].astype(jnp.float32)
            return acc + a * a + b * b

        acc = lax.fori_loop(0, n_chunks, squares, jnp.zeros((count, CHUNK), jnp.float32))
        scale = lax.rsqrt(jnp.sum(acc, axis=-1, keepdims=True) / features + 1e-05)

        def write(j, carry):
            for held, half in ((mine, side), (theirs, other)):
                where = cols(half * n_chunks + j)
                wide = held[j].astype(jnp.float32) * scale * gain[:, where]
                normed[held_rows, where] = wide.astype(jnp.bfloat16)
            return carry

        lax.fori_loop(0, n_chunks, write, 0)

    def keys_values(layer):
        count = layer_rows[layer]

        def one(n, carry):
            if layer == 0:
                kv_copy(n).wait()
            kv_cols[0:count, cols(n)] = jnp.dot(
                normed[0:count, :], kv_weights[n], preferred_element_type=jnp.float32
            ).astype(jnp.bfloat16)
            return carry

        lax.fori_loop(0, kv_chunks, one, 0)
        for which, keep in ((other, False), (side, True)):
            first = pl.multiple_of(which * own_kv * HD, own_kv * HD)
            heads = jnp.dot(
                kv_cols[0:count, :], spread[:, pl.ds(first, own_kv * HD)],
                preferred_element_type=jnp.float32,
            ).astype(jnp.bfloat16)
            for g in range(own_kv):
                if keep:
                    kv_heads[layer, side, g, 0:count] = heads[:, g * HD:(g + 1) * HD]
                else:
                    kv_send[layer, g, 0:count] = heads[:, g * HD:(g + 1) * HD]
            if not keep:
                kv_remote(layer).start()

    def query(layer, c):
        return jnp.dot(
            normed[0:layer_rows[layer], :], ring[lax.rem(c, SLOTS)], preferred_element_type=jnp.float32
        ).astype(jnp.bfloat16)

    def attend(layer, j, mine, first, count, allowed):
        here = slice(first, first + count)
        q = q_held[lax.rem(j, 2), here]
        g = j // group_chunks
        stacked = jnp.concatenate([q[:, i * HD:(i + 1) * HD] for i in range(chunk_heads)], axis=0)
        scores = lax.dot_general(
            stacked, kv_heads[layer, 0, g, here], (((1,), (1,)), ((), ())),
            preferred_element_type=jnp.float32,
        ) * HD ** (-0.5)
        e = jnp.where(allowed[...] > 0.0, jnp.exp(scores), 0.0)
        p = (e * (1.0 / jnp.sum(e, axis=-1, keepdims=True))).astype(jnp.bfloat16)
        a = jnp.dot(p, kv_heads[layer, 1, g, here], preferred_element_type=jnp.float32)
        side_by_side = jnp.concatenate(
            [a[i * count:(i + 1) * count] for i in range(chunk_heads)], axis=1
        )
        return (mine[j].astype(jnp.float32) + side_by_side).astype(jnp.bfloat16)

    def attend_all(layer, j):
        if layer == 0:
            return (attend(0, j, x_own, 0, rows, mask),)
        return (
            attend(1, j, next_own, 0, rows, mask),
            attend(1, j, early_own, rows, early_rows, early_mask),
        )

    def refill(c):
        @pl.when(c + SLOTS < total)
        def _():
            ring_copy(c + SLOTS).start()

    def run_layer(layer, finish):
        count = layer_rows[layer]
        base = layer * n_chunks
        ring_copy(base).wait()
        q_held[0, 0:count] = query(layer, base)
        refill(jnp.int32(base))
        kv_remote(layer).wait()

        def one(j, carry):
            c = base + j
            ring_copy(c).wait()
            fresh = query(layer, c)
            done = attend_all(layer, j - 1)
            q_held[lax.rem(j, 2), 0:count] = fresh
            refill(c)
            finish(j - 1, *done)
            return carry

        lax.fori_loop(1, n_chunks, one, 0)
        finish(n_chunks - 1, *attend_all(layer, n_chunks - 1))

    lag, early_lag = 4, 7

    def pass_on(j):
        h_remote(j).wait_recv()
        forward_remote(j).start()
        picked = jnp.dot(
            early_chooser[...], next_own[j], preferred_element_type=jnp.float32
        ).astype(jnp.bfloat16)
        for slot in range(half):
            early_send[j, slot] = picked[slot * capacity:(slot + 1) * capacity]
        for k in range(half):
            early_remote(k, j).start()

    def pass_early(j):
        for k in range(half):
            early_remote(k, j).wait_recv()
        early_forward(j).start()

    def send_next(j, done):
        h_send[j] = done
        h_remote(j).start()

        @pl.when(j >= lag)
        def _():
            pass_on(j - lag)

        @pl.when(j >= early_lag)
        def _():
            pass_early(j - early_lag)

    def send_docs(j, done, early):
        picked = jnp.dot(late_chooser[...], done, preferred_element_type=jnp.float32)
        picked = picked.astype(jnp.bfloat16)
        kept = jnp.where(valid[...] > 0.0, early.astype(jnp.float32), 0.0).astype(jnp.bfloat16)
        for slot in range(len(late_masks)):
            packed[slot, :, cols(j)] = picked[slot * capacity:(slot + 1) * capacity]
        for k in reversed(range(1, len(late_masks))):
            doc_remote(k, j).start()
        own_store(j).start()
        for slot in range(half):
            early_out[slot, :, cols(j)] = kept[slot * capacity:(slot + 1) * capacity]
        for slot in range(half):
            early_store(slot, j).start()

    fill_mask(meta)
    fill_early_mask()
    meta_remote().wait()
    for k in range(half):
        meta_on(k).start()
    fill_choosers(meta_next)
    for j in range(n_chunks):
        x_remote(j).wait()
    normalise(x_own, x_other, 0, rows)
    keys_values(0)
    run_layer(0, send_next)
    for j in range(n_chunks - lag, n_chunks):
        pass_on(j)
    fill_mask(meta_next)
    for k in range(half):
        meta_on(k).wait()
    fill_valid()
    for j in range(n_chunks - early_lag, n_chunks):
        pass_early(j)
    for j in range(n_chunks):
        forward_remote(j).wait()
    normalise(next_own, next_other, 0, rows)
    for j in range(n_chunks):
        early_forward(j).wait()
    normalise(early_own, early_other, rows, early_rows)
    keys_values(1)
    run_layer(1, send_docs)
    for j in range(n_chunks):
        h_remote(j).wait_send()
        for k in range(half):
            early_remote(k, j).wait_send()
    for slot in range(half):
        early_stored(slot).wait()
    own_stored().wait()
    for k in range(1, len(late_masks)):
        doc_all(k).wait()


def fused_device(sizes, hidden, doc_lengths, doc_target, norm_gain, q_weight, kv_weight):
    n_dp, n_pipe, docs = sizes
    rows, width = hidden.shape[1:]
    features = norm_gain.shape[1]
    n_chunks = width // CHUNK
    n_kv = kv_weight.shape[2]
    kv_chunks = n_kv // CHUNK
    own_kv = KV_HEADS // 2
    capacity = rows // 4
    chunk_heads = CHUNK // HD
    bf16 = jnp.bfloat16
    dma = pltpu.SemaphoreType.DMA
    vmem = pltpu.VMEM
    early_masks, late_masks = split_masks(n_dp)
    half, n_late = len(early_masks), len(late_masks)
    early_rows = half * capacity
    most = rows + early_rows
    blocks = vmem((n_chunks, rows, CHUNK), bf16)
    early_blocks = vmem((n_chunks, early_rows, CHUNK), bf16)
    result = pl.pallas_call(
        functools.partial(fused_kernel, sizes),
        out_shape=jax.ShapeDtypeStruct((n_dp * capacity, width), bf16),
        in_specs=[
            pl.BlockSpec(memory_space=pl.ANY),
            pl.BlockSpec(memory_space=pltpu.VMEM),
            pl.BlockSpec(memory_space=pltpu.VMEM),
            pl.BlockSpec(memory_space=pltpu.VMEM),
            pl.BlockSpec(memory_space=pl.ANY),
            pl.BlockSpec(memory_space=pl.ANY),
        ],
        out_specs=pl.BlockSpec(memory_space=pl.ANY),
        scratch_shapes=[
            vmem((8, 128), jnp.int32),
            blocks, blocks, blocks, blocks, blocks, early_blocks, early_blocks,
            vmem((n_chunks, half, capacity, CHUNK), bf16),
            vmem((8, 128), jnp.int32),
            vmem((half, 8, 128), jnp.int32),
            vmem((most, features), bf16),
            vmem((n_kv, n_kv), bf16),
            vmem((most, n_kv), bf16),
            vmem((STEPS, own_kv, most, HD), bf16),
            vmem((STEPS, 2, own_kv, most, HD), bf16),
            vmem((kv_chunks, features, CHUNK), bf16),
            vmem((SLOTS, features, CHUNK), bf16),
            vmem((chunk_heads * rows, rows), jnp.float32),
            vmem((chunk_heads * early_rows, early_rows), jnp.float32),
            vmem((early_rows, CHUNK), jnp.float32),
            vmem((early_rows, rows), bf16),
            vmem((n_late * capacity, rows), bf16),
            vmem((2, most, CHUNK), bf16),
            vmem((n_late, capacity, width), bf16),
            vmem((half, capacity, width), bf16),
            dma((n_chunks,)), dma((n_chunks,)), dma((n_chunks,)), dma, dma,
            dma((kv_chunks,)), dma((SLOTS,)), dma((STEPS,)), dma((STEPS,)),
            dma((n_chunks,)), dma((n_chunks,)), dma((n_chunks,)), dma((n_chunks,)),
            dma((n_late,)), dma((n_late,)), dma((half + 1,)),
            dma((half, n_chunks)), dma((half, n_chunks)), dma((n_chunks,)), dma((n_chunks,)),
            dma((half,)), dma((half,)),
        ],
        compiler_params=pltpu.CompilerParams(
            collective_id=0, has_side_effects=True, vmem_limit_bytes=67043328
        ),
    )(hidden[0], doc_lengths[0], doc_target[0], norm_gain, q_weight[0], kv_weight[0])
    return result[None]


def solution(mesh):
    placed = (
        P("pipe", "dp", "tensor"),
        P("pipe", "dp", None),
        P("pipe", "dp", None),
        P("pipe", None),
        P("pipe", None, "tensor"),
        P("pipe", None, "tensor"),
    )
    run = on_device
    if mesh.shape["tensor"] == 2 and mesh.shape["dp"] in (4, 8, 16):
        sizes = (mesh.shape["dp"], mesh.shape["pipe"], mesh.shape["dp"])
        run = functools.partial(fused_device, sizes)
    return jax.shard_map(
        run, mesh=mesh, in_specs=placed, out_specs=P("pipe", "dp", "tensor"), check_vma=False
    )
```
